32 devices in a mesh: ev: 16 (over z, y, core), st: 2 (over x).
Axes of the slice: x: 2, y: 2, z: 4, core: 2. Of those that a mesh axis runs over, the one named last changes fastest.
Arguments:
- strain: bfloat16 [2, 6, 256, 4096], P(None, None, 'ev'), may hold values from -0.068359375 to 0.068359375
- green: bfloat16 [2, 3, 256, 6, 4096], P(None, None, 'st', None, 'ev'), may hold values from -6 to 6
- weights: bfloat16 [2, 3, 256, 256], P(None, None, 'ev', 'st'), may hold values from -0.15625 to 0.15625
- mask: int32 [256, 256], P('ev', 'st'), may hold values 0 or 1
Outputs:
- kernels: float32 [2, 4096], P(None, ('ev', 'st'))
The draws below stay inside these ranges and needn't reach their ends.
All inputs are finite; a program needn't handle non-finite values. No bound on the sum of `mask` on one device may be relied on, other than what follows from the above.
Results may differ from the reference program's by a relative error of at most 0.0003.
Values may be sent and summed in bfloat16 or wider, within the bound.
No kernel may reach another device: no remote copies, remote signals or barrier semaphores. Data moves between devices by JAX's collectives and lax.ppermute only.
A program may use at most 128 MiB of HBM per device.

```python
import jax
import jax.numpy as jnp
from jax import lax

XI = 256
EV = 256
ST = 256
X = 4096


def set_ends(values, key, least, high):
    longest = values.shape.index(max(values.shape))
    spots = []
    for shift in (0, 1):
        where = [jax.random.randint(jax.random.fold_in(key, axis), (), 0, length) for axis, length in enumerate(values.shape)]
        where[longest] = (where[longest] + shift) % values.shape[longest]
        spots.append(tuple(where))
    return values.at[spots[0]].set(least).at[spots[1]].set(high)


def strengthened(entries, rng, source, target, shards_of, factor):
    def block_of(position):
        return (jnp.arange(entries.shape[position]) // (entries.shape[position] // shards_of)).reshape((-1,) + (1,) * (entries.ndim - 1 - position))

    one_side = jax.random.permutation(rng, shards_of)[block_of(target)]
    other_side = (block_of(target) + shards_of // 2) % shards_of
    return jnp.where((block_of(source) == one_side) | (block_of(source) == other_side), factor * entries, entries)


def levels(rng, dims, cuts, low, largest):
    gain = 1.0
    for dim, parts in cuts:
        draws = jax.random.uniform(jax.random.fold_in(jax.random.fold_in(rng, 6), dim), (parts,), jnp.float32, low / len(cuts), largest / len(cuts))
        gain = gain * jnp.repeat(jnp.exp(draws), dims[dim] // parts).reshape((-1,) + (1,) * (len(dims) - 1 - dim))
    return gain


def bell_draw(key, dims, width, limit, shards=(), held_as=jnp.bfloat16):
    loudness = levels(key, dims, shards, -0.22, 0.18) if shards else 1.0
    values = jax.random.normal(key, dims, jnp.float32) * width * loudness
    return jnp.minimum(jnp.maximum(values, -limit), limit).astype(held_as)


def heavy_noise(own_key, dims, spread, most, shards, heavy, kind=jnp.bfloat16):
    result = spread * jax.random.normal(own_key, dims, jnp.float32)
    if shards:
        result = result * levels(own_key, dims, shards, -0.22, 0.18)
    return jnp.clip(strengthened(result, jax.random.fold_in(own_key, 3), *heavy), -most, most).astype(kind)


def setup_inputs(seed: int = 0) -> dict:
    keys = jax.random.split(jax.random.key(seed), 5)
    return {
        "strain": bell_draw(keys[0], (2, 6, EV, X), (1.0 / (30 * EV) ** 0.5), 0.068359375, ((2, 16),)),
        "green": heavy_noise(keys[1], (2, 3, ST, 6, X), 1.0, 6.0, ((2, 2), (4, 16)), (2, 4, 16, 2.0)),
        "weights": bell_draw(keys[2], (2, 3, EV, ST), (6 * ST) ** -0.5, 0.15625, ((2, 16), (3, 2))),
        "mask": set_ends((jax.random.randint(keys[3], (EV, ST), 0, 4) < 3).astype(jnp.int32), jax.random.fold_in(keys[3], 1), 0, 1),
    }


def reference(strain, green, weights, mask):
    weighted = (weights * mask.astype(jnp.bfloat16)[None, None]).astype(jnp.float32)
    voigt = jnp.array([1.0, 1.0, 1.0, 2.0, 2.0, 2.0], jnp.float32)

    def one_block(block_index):
        first_cell = (block_index * XI).astype(jnp.int32)
        green_block = lax.dynamic_slice_in_dim(green, first_cell, XI, 4).astype(jnp.float32)
        strain_block = lax.dynamic_slice_in_dim(strain, first_cell, XI, 3).astype(jnp.float32)
        products = jnp.einsum("rfes,qfscx->rqecx", weighted, green_block, precision=lax.Precision.HIGHEST)
        held_real = products[0, 0] - products[1, 1]
        held_imag = products[0, 1] + products[1, 0]
        strain_real = jnp.swapaxes(strain_block[0], 0, 1)
        strain_imag = jnp.swapaxes(strain_block[1], 0, 1)
        trace_term = jnp.sum(strain_real[:, :3].sum(1) * held_real[:, :3].sum(1) - strain_imag[:, :3].sum(1) * held_imag[:, :3].sum(1), axis=0)
        shear_term = jnp.sum((strain_real * held_real - strain_imag * held_imag) * voigt[None, :, None], axis=(0, 1))
        return jnp.stack([trace_term, shear_term])

    blocks = lax.map(one_block, jnp.arange(X // XI, dtype=jnp.int32))
    return jnp.transpose(blocks, (1, 0, 2)).reshape(2, X)
```

```python
import functools

import jax
import jax.numpy as jnp
from jax import lax
from jax.experimental import pallas as pl
from jax.experimental.pallas import tpu as pltpu
from jax.sharding import PartitionSpec as P

LANES = 128
COMPONENTS = 6


def general(strain, green, weights, mask):
    masked = weights * mask.astype(jnp.bfloat16)[None, None]
    cells_dev = green.shape[4]
    station_count = green.shape[2]
    event_rows = strain.shape[2]
    ev_count = lax.axis_size("ev")
    st_count = lax.axis_size("st")
    sub_cells = cells_dev // st_count
    shaped = strain.reshape(2, 6, event_rows, ev_count, st_count, sub_cells)
    selected = lax.dynamic_index_in_dim(shaped, lax.axis_index("st"), 4, keepdims=False)
    selected = selected.reshape(2, 6, event_rows, ev_count * sub_cells)
    narrow = lax.all_to_all(selected, "ev", split_axis=3, concat_axis=2, tiled=True)
    strain_all = lax.all_gather(narrow, "st", axis=3, tiled=True)
    green_flat = green.reshape(2, 3, station_count, 6 * cells_dev)
    voigt = jnp.array([1.0, 1.0, 1.0, 2.0, 2.0, 2.0], jnp.float32)
    weight_rows = lax.all_gather(masked, "ev", axis=2, tiled=True)
    row_count = weight_rows.shape[2]
    products = jnp.einsum(
        "rfps,qfsn->rqpn", weight_rows, green_flat, preferred_element_type=jnp.float32
    )
    held_real = (products[0, 0] - products[1, 1]).reshape(row_count, 6, cells_dev)
    held_imag = (products[0, 1] + products[1, 0]).reshape(row_count, 6, cells_dev)
    strain_rows = strain_all.astype(jnp.float32)
    strain_real = jnp.swapaxes(strain_rows[0], 0, 1)
    strain_imag = jnp.swapaxes(strain_rows[1], 0, 1)
    trace_term = jnp.sum(
        strain_real[:, :3].sum(1) * held_real[:, :3].sum(1)
        - strain_imag[:, :3].sum(1) * held_imag[:, :3].sum(1),
        axis=0,
    )
    shear_term = jnp.sum(
        (strain_real * held_real - strain_imag * held_imag) * voigt[None, :, None], axis=(0, 1)
    )
    partial_value = jnp.stack([trace_term, shear_term])
    return lax.psum_scatter(partial_value, "st", scatter_dimension=1, tiled=True)


def green_slice_kernel(side_ref, x_ref, o_ref, buf, in_sem, out_sem):
    parts = in_sem.shape[0]
    size = x_ref.shape[0] // parts
    lane = pl.multiple_of((1 - side_ref[0]) * LANES, LANES)

    def take(i):
        return pltpu.make_async_copy(
            x_ref.at[pl.ds(i * size, size), :, pl.ds(lane, LANES)],
            buf.at[pl.ds(i * size, size)],
            in_sem.at[i],
        )

    def give(i):
        return pltpu.make_async_copy(
            buf.at[pl.ds(i * size, size)], o_ref.at[pl.ds(i * size, size)], out_sem.at[i]
        )

    for i in range(parts):
        take(i).start()
    for i in range(parts):
        take(i).wait()
        give(i).start()
    for i in range(parts):
        give(i).wait()


def green_slice(side, green):
    rows, stations, _ = green.shape
    parts = 4
    return pl.pallas_call(
        green_slice_kernel,
        out_shape=jax.ShapeDtypeStruct((rows, stations, LANES), green.dtype),
        in_specs=[
            pl.BlockSpec(memory_space=pltpu.SMEM),
            pl.BlockSpec(memory_space=pl.ANY),
        ],
        out_specs=pl.BlockSpec(memory_space=pl.ANY),
        scratch_shapes=[
            pltpu.VMEM((rows, stations, LANES), green.dtype),
            pltpu.SemaphoreType.DMA((parts,)),
            pltpu.SemaphoreType.DMA((parts,)),
        ],
        cost_estimate=pl.CostEstimate(flops=0, bytes_accessed=4 * rows * stations * LANES, transcendentals=0),
        name="green_slice",
    )(side, green)


def strain_slice_kernel(count, st_count, side_ref, x_ref, o_ref, buf, in_sem, out_sem):
    def take(i):
        lane = pl.multiple_of((i * st_count + side_ref[0]) * LANES, LANES)
        return pltpu.make_async_copy(x_ref.at[:, :, pl.ds(lane, LANES)], buf.at[i], in_sem.at[i])

    def give(i):
        return pltpu.make_async_copy(buf.at[i], o_ref.at[i], out_sem.at[i])

    for i in range(count):
        take(i).start()
    for i in range(count):
        take(i).wait()
        give(i).start()
    for i in range(count):
        give(i).wait()


def strain_slice(side, strain, ev_count, st_count):
    rows, events, _ = strain.shape
    return pl.pallas_call(
        functools.partial(strain_slice_kernel, ev_count, st_count),
        out_shape=jax.ShapeDtypeStruct((ev_count, rows, events, LANES), strain.dtype),
        in_specs=[
            pl.BlockSpec(memory_space=pltpu.SMEM),
            pl.BlockSpec(memory_space=pl.ANY),
        ],
        out_specs=pl.BlockSpec(memory_space=pl.ANY),
        scratch_shapes=[
            pltpu.VMEM((ev_count, rows, events, LANES), strain.dtype),
            pltpu.SemaphoreType.DMA((ev_count,)),
            pltpu.SemaphoreType.DMA((ev_count,)),
        ],
        cost_estimate=pl.CostEstimate(
            flops=0, bytes_accessed=4 * ev_count * rows * events * LANES, transcendentals=0
        ),
        name="strain_slice",
    )(side, strain)


def held_kernel(order_ref, w_ref, own_ref, other_ref, o_ref, lhs):
    count, _, _, _, events, stations = w_ref.shape

    @pl.when(pl.program_id(0) == 0)
    def _():
        for t in range(count):
            block = w_ref[order_ref[t]]
            for h in range(2):
                for r in range(2):
                    for f in range(3):
                        column = ((h * 2 + r) * 3 + f) * stations
                        lhs[t * events : (t + 1) * events, column : column + stations] = block[h, r, f]

    total = None
    for h, g_ref in enumerate((own_ref, other_ref)):
        real = g_ref[0, :, 0].reshape(3 * stations, LANES)
        imag = g_ref[1, :, 0].reshape(3 * stations, LANES)
        upper = jnp.concatenate([real, imag], axis=1)
        lower = jnp.concatenate([-imag, real], axis=1)
        rhs = jnp.concatenate([upper, lower], axis=0)
        width = 6 * stations
        part = jnp.dot(lhs[:, h * width : (h + 1) * width], rhs, preferred_element_type=jnp.float32)
        total = part if total is None else total + part
    o_ref[0] = total


def held_product(side, order, weights, green, other):
    count, _, _, _, events, stations = weights.shape
    spec = pltpu.PrefetchScalarGridSpec(
        num_scalar_prefetch=2,
        grid=(COMPONENTS,),
        in_specs=[
            pl.BlockSpec(weights.shape, lambda c, order, side: (0,) * 6),
            pl.BlockSpec((2, 3, 1, stations, LANES), lambda c, order, side: (0, 0, c, 0, side[0])),
            pl.BlockSpec((2, 3, 1, stations, LANES), lambda c, order, side: (0, 0, c, 0, 0)),
        ],
        out_specs=pl.BlockSpec((1, count * events, 2 * LANES), lambda c, order, side: (c, 0, 0)),
        scratch_shapes=[pltpu.VMEM((count * events, 12 * stations), jnp.bfloat16)],
    )

    def body(order_ref, side_ref, *refs):
        held_kernel(order_ref, *refs)

    return pl.pallas_call(
        body,
        grid_spec=spec,
        out_shape=jax.ShapeDtypeStruct((COMPONENTS, count * events, 2 * LANES), jnp.float32),
        cost_estimate=pl.CostEstimate(
            flops=2 * COMPONENTS * count * events * 12 * stations * 2 * LANES,
            bytes_accessed=COMPONENTS * (count * events * LANES * 8 + stations * LANES * 24),
            transcendentals=0,
        ),
        name="held_product",
    )(order, side, weights, green, other)


def combine_kernel(strain_ref, held_ref, o_ref):
    blocks, _, events, _ = strain_ref.shape

    @pl.when(pl.program_id(0) == 0)
    def _():
        o_ref[...] = jnp.zeros_like(o_ref)

    trace = jnp.zeros((events, LANES), jnp.float32)
    normal = jnp.zeros((events, LANES), jnp.float32)
    cross = jnp.zeros((events, LANES), jnp.float32)
    for b in range(blocks):
        rows = slice(b * events, (b + 1) * events)
        sums = None
        for c in range(COMPONENTS):
            real = strain_ref[b, c].astype(jnp.float32)
            imag = strain_ref[b, COMPONENTS + c].astype(jnp.float32)
            held_real = held_ref[c, rows, :LANES]
            held_imag = held_ref[c, rows, LANES:]
            term = real * held_real - imag * held_imag
            if c < 3:
                normal = normal + term
                four = (real, imag, held_real, held_imag)
                sums = four if sums is None else tuple(x + y for x, y in zip(sums, four))
            else:
                cross = cross + term
        trace = trace + (sums[0] * sums[2] - sums[1] * sums[3])
    shear = normal + 2.0 * cross
    o_ref[0:1, :] += jnp.sum(trace, axis=0, keepdims=True)
    o_ref[1:2, :] += jnp.sum(shear, axis=0, keepdims=True)


def combine(strain, held):
    count, rows, events, _ = strain.shape
    steps = 4 if count % 4 == 0 else 1
    blocks = count // steps
    return pl.pallas_call(
        combine_kernel,
        grid=(steps,),
        in_specs=[
            pl.BlockSpec((blocks, rows, events, LANES), lambda i: (i, 0, 0, 0)),
            pl.BlockSpec((COMPONENTS, blocks * events, 2 * LANES), lambda i: (0, i, 0)),
        ],
        out_specs=pl.BlockSpec((2, LANES), lambda i: (0, 0)),
        out_shape=jax.ShapeDtypeStruct((2, LANES), jnp.float32),
        cost_estimate=pl.CostEstimate(
            flops=count * events * LANES * 50,
            bytes_accessed=count * events * LANES * (24 + 48),
            transcendentals=0,
        ),
        name="combine",
    )(strain, held)


def paired(strain, green, weights, mask):
    ev_count = lax.axis_size("ev")
    st_count = lax.axis_size("st")
    event_rows = strain.shape[2]
    station_count = green.shape[2]
    me = lax.axis_index("ev").astype(jnp.int32)
    side = lax.axis_index("st").astype(jnp.int32)[None]
    swap = [(0, 1), (1, 0)]

    green = jnp.transpose(green, (0, 1, 3, 2, 4))
    with jax.named_scope("green_swap"):
        flat = green.reshape(36, station_count, 2 * LANES)
        sent = green_slice(side, flat)
        other = lax.ppermute(sent, "st", swap).reshape(2, 3, 6, station_count, LANES)

    with jax.named_scope("weights_swap"):
        masked = weights * mask.astype(jnp.bfloat16)[None, None]
        both = jnp.stack([masked, lax.ppermute(masked, "st", swap)])

    with jax.named_scope("strain_move"):
        pieces = strain_slice(side, strain.reshape(12, event_rows, -1), ev_count, st_count)
        moved = lax.all_to_all(pieces, "ev", 0, 0, tiled=True)

    gathered = both[None]
    bits = []
    bit = ev_count // 2
    while bit:
        with jax.named_scope(f"weights_{bit}"):
            got = lax.ppermute(gathered, "ev", [(i, i ^ bit) for i in range(ev_count)])
            gathered = jnp.concatenate([gathered, got], 0)
        bits.append(bit)
        bit //= 2
    positions = []
    for x in range(ev_count):
        positions.append(sum(1 << k for k, b in enumerate(bits) if x & b))
    offsets = jnp.arange(ev_count, dtype=jnp.int32) ^ me
    order = sum(((offsets & b) // b) << k for k, b in enumerate(bits))

    held = held_product(side, order.astype(jnp.int32), gathered, green, other)
    return combine(moved, held)


def local(strain, green, weights, mask):
    ev_count = lax.axis_size("ev")
    st_count = lax.axis_size("st")
    fits = (
        st_count == 2
        and ev_count & (ev_count - 1) == 0
        and green.shape[4] == st_count * LANES
        and green.shape[2] % LANES == 0
        and strain.shape[2] % 16 == 0
    )
    return (paired if fits else general)(strain, green, weights, mask)


def solution(mesh):
    placed = (
        P(None, None, "ev", None),
        P(None, None, "st", None, "ev"),
        P(None, None, "ev", "st"),
        P("ev", "st"),
    )
    return jax.shard_map(
        local, mesh=mesh, in_specs=placed, out_specs=P(None, ("ev", "st")), check_vma=False
    )
```

```python
import functools

import jax
import jax.numpy as jnp
from jax import lax
from jax.experimental import pallas as pl
from jax.experimental.pallas import tpu as pltpu
from jax.sharding import PartitionSpec as P

LANES = 128
COMPONENTS = 6


def general(strain, green, weights, mask):
    masked = weights * mask.astype(jnp.bfloat16)[None, None]
    cells_dev = green.shape[4]
    station_count = green.shape[2]
    event_rows = strain.shape[2]
    ev_count = lax.axis_size("ev")
    st_count = lax.axis_size("st")
    sub_cells = cells_dev // st_count
    shaped = strain.reshape(2, 6, event_rows, ev_count, st_count, sub_cells)
    selected = lax.dynamic_index_in_dim(shaped, lax.axis_index("st"), 4, keepdims=False)
    selected = selected.reshape(2, 6, event_rows, ev_count * sub_cells)
    narrow = lax.all_to_all(selected, "ev", split_axis=3, concat_axis=2, tiled=True)
    strain_all = lax.all_gather(narrow, "st", axis=3, tiled=True)
    green_flat = green.reshape(2, 3, station_count, 6 * cells_dev)
    voigt = jnp.array([1.0, 1.0, 1.0, 2.0, 2.0, 2.0], jnp.float32)
    weight_rows = lax.all_gather(masked, "ev", axis=2, tiled=True)
    row_count = weight_rows.shape[2]
    products = jnp.einsum(
        "rfps,qfsn->rqpn", weight_rows, green_flat, preferred_element_type=jnp.float32
    )
    held_real = (products[0, 0] - products[1, 1]).reshape(row_count, 6, cells_dev)
    held_imag = (products[0, 1] + products[1, 0]).reshape(row_count, 6, cells_dev)
    strain_rows = strain_all.astype(jnp.float32)
    strain_real = jnp.swapaxes(strain_rows[0], 0, 1)
    strain_imag = jnp.swapaxes(strain_rows[1], 0, 1)
    trace_term = jnp.sum(
        strain_real[:, :3].sum(1) * held_real[:, :3].sum(1)
        - strain_imag[:, :3].sum(1) * held_imag[:, :3].sum(1),
        axis=0,
    )
    shear_term = jnp.sum(
        (strain_real * held_real - strain_imag * held_imag) * voigt[None, :, None], axis=(0, 1)
    )
    partial_value = jnp.stack([trace_term, shear_term])
    return lax.psum_scatter(partial_value, "st", scatter_dimension=1, tiled=True)


VMEM_LIMIT = 24 * 1024 * 1024
GREEN_LIMIT = 64_700_000
VMEM_ALL = 65_800_000


def params(limit=VMEM_LIMIT):
    return pltpu.CompilerParams(vmem_limit_bytes=limit)


def in_vmem():
    return pl.BlockSpec(memory_space=pltpu.VMEM)


def in_smem():
    return pl.BlockSpec(memory_space=pltpu.SMEM)


def in_hbm():
    return pl.BlockSpec(memory_space=pltpu.HBM)


def green_copies(green_ref, buf, sems, first, lane):
    triple = buf.shape[1]
    return [
        pltpu.make_async_copy(
            green_ref.at[i, pl.ds(first, triple), :, pl.ds(lane, LANES)], buf.at[i], sems.at[i]
        )
        for i in range(buf.shape[0])
    ]


def first_kernel(
    side_ref, green_ref, weights_ref, mask_ref,
    sent_ref, masked_ref, buf, weights_buf, mask_buf, sems, small_sems, out_sem,
):
    lane = pl.multiple_of((1 - side_ref[0]) * LANES, LANES)
    small = [
        pltpu.make_async_copy(weights_ref, weights_buf, small_sems.at[0]),
        pltpu.make_async_copy(mask_ref, mask_buf, small_sems.at[1]),
    ]
    copies = green_copies(green_ref, buf, sems, 0, lane)
    for copy in small + copies:
        copy.start()
    for copy in small:
        copy.wait()
    keep = mask_buf[...].astype(jnp.bfloat16)
    for r in range(2):
        for f in range(3):
            masked_ref[r, f] = weights_buf[r, f] * keep
    for copy in copies:
        copy.wait()
    give = pltpu.make_async_copy(buf, sent_ref, out_sem)
    give.start()
    give.wait()


def first_pieces(side, green, weights, mask):
    rows, _, stations, _ = green.shape
    shape = (rows, COMPONENTS // 2, stations, LANES)
    return pl.pallas_call(
        first_kernel,
        out_shape=(
            jax.ShapeDtypeStruct(shape, green.dtype),
            jax.ShapeDtypeStruct(weights.shape, weights.dtype),
        ),
        in_specs=[in_smem(), in_hbm(), in_hbm(), in_hbm()],
        out_specs=(in_hbm(), in_vmem()),
        scratch_shapes=[
            pltpu.VMEM(shape, green.dtype),
            pltpu.VMEM(weights.shape, weights.dtype),
            pltpu.VMEM(mask.shape, mask.dtype),
            pltpu.SemaphoreType.DMA((rows,)),
            pltpu.SemaphoreType.DMA((2,)),
            pltpu.SemaphoreType.DMA,
        ],
        compiler_params=params(VMEM_ALL),
        name="first_pieces",
    )(side, green, weights, mask)


def green_kernel(side_ref, green_ref, sent_ref, buf, sems, out_sem):
    lane = pl.multiple_of((1 - side_ref[0]) * LANES, LANES)
    copies = green_copies(green_ref, buf, sems, COMPONENTS // 2, lane)
    for copy in copies:
        copy.start()
    for copy in copies:
        copy.wait()
    give = pltpu.make_async_copy(buf, sent_ref, out_sem)
    give.start()
    give.wait()


def green_pieces(side, green):
    rows, _, stations, _ = green.shape
    shape = (rows, COMPONENTS // 2, stations, LANES)
    return pl.pallas_call(
        green_kernel,
        out_shape=jax.ShapeDtypeStruct(shape, green.dtype),
        in_specs=[in_smem(), in_hbm()],
        out_specs=in_hbm(),
        scratch_shapes=[
            pltpu.VMEM(shape, green.dtype),
            pltpu.SemaphoreType.DMA((rows,)),
            pltpu.SemaphoreType.DMA,
        ],
        compiler_params=params(GREEN_LIMIT),
        name="green_pieces",
    )(side, green)


def strain_kernel(st_count, side_ref, strain_ref, pieces_ref, buf, sems, out_sems):
    count = pieces_ref.shape[0]
    takes, gives = [], []
    for i in range(count):
        lane = pl.multiple_of((i * st_count + side_ref[0]) * LANES, LANES)
        takes.append(
            pltpu.make_async_copy(strain_ref.at[:, :, pl.ds(lane, LANES)], buf.at[i], sems.at[i])
        )
    groups = out_sems.shape[0]
    size = count // groups
    for g in range(groups):
        part = pl.ds(g * size, size)
        gives.append(pltpu.make_async_copy(buf.at[part], pieces_ref.at[part], out_sems.at[g]))
    for copy in takes:
        copy.start()
    for g in range(groups):
        for copy in takes[g * size : (g + 1) * size]:
            copy.wait()
        gives[g].start()
    for copy in gives:
        copy.wait()


def strain_pieces(side, strain, ev_count, st_count):
    parts, events, _ = strain.shape
    shape = (ev_count, parts, events, LANES)
    return pl.pallas_call(
        functools.partial(strain_kernel, st_count),
        out_shape=jax.ShapeDtypeStruct(shape, strain.dtype),
        in_specs=[in_smem(), in_hbm()],
        out_specs=in_hbm(),
        scratch_shapes=[
            pltpu.VMEM(shape, strain.dtype),
            pltpu.SemaphoreType.DMA((ev_count,)),
            pltpu.SemaphoreType.DMA((4,)),
        ],
        compiler_params=params(VMEM_ALL),
        name="strain_pieces",
    )(side, strain)


def stacked(block_ref, components, lane=0):
    columns = []
    for c in components:
        columns.append(
            jnp.concatenate(
                [block_ref[i, c, :, pl.ds(lane, LANES)] for i in range(block_ref.shape[0])], axis=0
            )
        )
    return columns[0] if len(columns) == 1 else jnp.concatenate(columns, axis=1)


def product(left, right):
    return jnp.dot(left, right, preferred_element_type=jnp.float32)


def held_kernel(me_ref, side_ref, near_ref, y_ref, core_ref, both_ref, green_ref, other_ref, held_ref, before_ref, lhs_ref):
    quads = (near_ref, core_ref, y_ref, both_ref)
    _, far, _, _, events, stations = near_ref.shape
    count = len(quads) * far
    half = count * events
    for x in range(count):
        z, bit, place = 0, count // 2, 0
        while bit > 2:
            z += ((x // bit) & 1) << place
            bit, place = bit // 2, place + 1
        w_ref = quads[x & 3]
        start = pl.multiple_of((me_ref[0] ^ x) * events, events)
        rows = pl.ds(start, events)
        low = pl.ds(start + half, events)
        for h in range(2):
            for f in range(3):
                real = w_ref[h, z, 0, f]
                imag = w_ref[h, z, 1, f]
                first = slice(f * stations, (f + 1) * stations)
                second = slice((3 + f) * stations, (4 + f) * stations)
                lhs_ref[h, rows, first] = real
                lhs_ref[h, low, first] = imag
                lhs_ref[h, rows, second] = -imag
                lhs_ref[h, low, second] = real
    lane = pl.multiple_of(side_ref[0] * LANES, LANES)
    wide = 2 * LANES
    held_ref[:, :wide] = product(lhs_ref[0], stacked(green_ref, (0, 1), lane)) + product(
        lhs_ref[1], stacked(other_ref, (0, 1))
    )
    middle = product(lhs_ref[0], stacked(green_ref, (2, 3), lane))
    held_ref[:, wide:] = middle[:, :LANES] + product(lhs_ref[1], stacked(other_ref, (2,)))
    before_ref[:, :LANES] = middle[:, LANES:]
    before_ref[:, LANES:] = product(lhs_ref[0], stacked(green_ref, (4, 5), lane))


def held_first(me, side, near, y, core, both, green, other):
    _, far, _, _, events, stations = near.shape
    rows = 8 * far * events
    return pl.pallas_call(
        held_kernel,
        out_shape=(
            jax.ShapeDtypeStruct((rows, COMPONENTS // 2 * LANES), jnp.float32),
            jax.ShapeDtypeStruct((rows, COMPONENTS // 2 * LANES), jnp.float32),
            jax.ShapeDtypeStruct((2, rows, 6 * stations), jnp.bfloat16),
        ),
        in_specs=[in_smem(), in_smem()] + [in_vmem()] * 6,
        out_specs=(in_vmem(),) * 3,
        compiler_params=params(),
        name="held_first",
    )(me, side, near, y, core, both, green, other)


def rest_kernel(lhs_ref, other_ref, before_ref, rest_ref):
    rest_ref[:, :LANES] = before_ref[:, :LANES] + product(lhs_ref[1], stacked(other_ref, (0,)))
    rest_ref[:, LANES:] = before_ref[:, LANES:] + product(lhs_ref[1], stacked(other_ref, (1, 2)))


def held_rest(lhs, other, before):
    return pl.pallas_call(
        rest_kernel,
        out_shape=jax.ShapeDtypeStruct(before.shape, before.dtype),
        in_specs=[in_vmem()] * 3,
        out_specs=in_vmem(),
        compiler_params=params(),
        name="held_rest",
    )(lhs, other, before)


def combine_kernel(strain_ref, first_ref, rest_ref, o_ref):
    blocks, _, events, _ = strain_ref.shape
    half = blocks * events
    trace = jnp.zeros((events, LANES), jnp.float32)
    normal = jnp.zeros((events, LANES), jnp.float32)
    cross = jnp.zeros((events, LANES), jnp.float32)
    for b in range(blocks):
        rows = slice(b * events, (b + 1) * events)
        low = slice(half + b * events, half + (b + 1) * events)
        sums = None
        for c in range(COMPONENTS):
            held_ref = first_ref if c < 3 else rest_ref
            lanes = slice((c % 3) * LANES, (c % 3 + 1) * LANES)
            real = strain_ref[b, c].astype(jnp.float32)
            imag = strain_ref[b, COMPONENTS + c].astype(jnp.float32)
            held_real = held_ref[rows, lanes]
            held_imag = held_ref[low, lanes]
            term = real * held_real - imag * held_imag
            if c < 3:
                normal = normal + term
                four = (real, imag, held_real, held_imag)
                sums = four if sums is None else tuple(x + y for x, y in zip(sums, four))
            else:
                cross = cross + term
        trace = trace + (sums[0] * sums[2] - sums[1] * sums[3])
    shear = normal + 2.0 * cross
    o_ref[0:1, :] = jnp.sum(trace, axis=0, keepdims=True)
    o_ref[1:2, :] = jnp.sum(shear, axis=0, keepdims=True)


def combine(strain, first, rest):
    return pl.pallas_call(
        combine_kernel,
        out_shape=jax.ShapeDtypeStruct((2, LANES), jnp.float32),
        in_specs=[in_vmem()] * 3,
        out_specs=in_vmem(),
        compiler_params=params(),
        name="combine",
    )(strain, first, rest)


def paired(strain, green, weights, mask):
    return paired_steps(strain, green, weights, mask)


def paired_steps(strain, green, weights, mask):
    ev_count = lax.axis_size("ev")
    st_count = lax.axis_size("st")
    event_rows = strain.shape[2]
    station_count = green.shape[2]
    me = lax.axis_index("ev").astype(jnp.int32)[None]
    side = lax.axis_index("st").astype(jnp.int32)[None]

    def hop(x, bit):
        return lax.ppermute(x, "ev", [(i, i ^ bit) for i in range(ev_count)])

    def swap(x):
        return lax.ppermute(x, "st", [(0, 1), (1, 0)])

    green = jnp.transpose(green, (0, 1, 3, 2, 4)).reshape(6, COMPONENTS, station_count, 2 * LANES)
    sent_first, masked = first_pieces(side, green, weights, mask)
    other_first = swap(sent_first)

    gathered = masked[None]
    bit = ev_count // 2
    while bit > 2:
        gathered = jnp.concatenate([gathered, hop(gathered, bit)])
        bit //= 2

    pieces = strain_pieces(side, strain.reshape(12, event_rows, -1), ev_count, st_count)
    moved = lax.all_to_all(pieces, "ev", 0, 0, tiled=True)

    near = jnp.stack([gathered, swap(gathered)])
    sent_rest = green_pieces(side, green)
    other_rest = swap(sent_rest)
    y = hop(near, 2)
    core = hop(near, 1)
    both = hop(y, 1)

    first, before, lhs = held_first(me, side, near, y, core, both, green, other_first)
    rest = held_rest(lhs, other_rest, before)
    return combine(moved, first, rest)


def local(strain, green, weights, mask):
    ev_count = lax.axis_size("ev")
    st_count = lax.axis_size("st")
    fits = (
        st_count == 2
        and ev_count >= 8
        and ev_count & (ev_count - 1) == 0
        and green.shape[4] == st_count * LANES
        and green.shape[2] % LANES == 0
        and strain.shape[2] % 16 == 0
    )
    return (paired if fits else general)(strain, green, weights, mask)


def solution(mesh):
    placed = (
        P(None, None, "ev", None),
        P(None, None, "st", None, "ev"),
        P(None, None, "ev", "st"),
        P("ev", "st"),
    )
    return jax.shard_map(
        local, mesh=mesh, in_specs=placed, out_specs=P(None, ("ev", "st")), check_vma=False
    )
```

```python
import functools

import jax
import jax.numpy as jnp
from jax import lax
from jax.experimental import pallas as pl
from jax.experimental.pallas import tpu as pltpu
from jax.sharding import PartitionSpec as P

LANES = 128
COMPONENTS = 6


def general(strain, green, weights, mask):
    masked = weights * mask.astype(jnp.bfloat16)[None, None]
    cells_dev = green.shape[4]
    station_count = green.shape[2]
    event_rows = strain.shape[2]
    ev_count = lax.axis_size("ev")
    st_count = lax.axis_size("st")
    sub_cells = cells_dev // st_count
    shaped = strain.reshape(2, 6, event_rows, ev_count, st_count, sub_cells)
    selected = lax.dynamic_index_in_dim(shaped, lax.axis_index("st"), 4, keepdims=False)
    selected = selected.reshape(2, 6, event_rows, ev_count * sub_cells)
    narrow = lax.all_to_all(selected, "ev", split_axis=3, concat_axis=2, tiled=True)
    strain_all = lax.all_gather(narrow, "st", axis=3, tiled=True)
    green_flat = green.reshape(2, 3, station_count, 6 * cells_dev)
    voigt = jnp.array([1.0, 1.0, 1.0, 2.0, 2.0, 2.0], jnp.float32)
    weight_rows = lax.all_gather(masked, "ev", axis=2, tiled=True)
    row_count = weight_rows.shape[2]
    products = jnp.einsum(
        "rfps,qfsn->rqpn", weight_rows, green_flat, preferred_element_type=jnp.float32
    )
    held_real = (products[0, 0] - products[1, 1]).reshape(row_count, 6, cells_dev)
    held_imag = (products[0, 1] + products[1, 0]).reshape(row_count, 6, cells_dev)
    strain_rows = strain_all.astype(jnp.float32)
    strain_real = jnp.swapaxes(strain_rows[0], 0, 1)
    strain_imag = jnp.swapaxes(strain_rows[1], 0, 1)
    trace_term = jnp.sum(
        strain_real[:, :3].sum(1) * held_real[:, :3].sum(1)
        - strain_imag[:, :3].sum(1) * held_imag[:, :3].sum(1),
        axis=0,
    )
    shear_term = jnp.sum(
        (strain_real * held_real - strain_imag * held_imag) * voigt[None, :, None], axis=(0, 1)
    )
    partial_value = jnp.stack([trace_term, shear_term])
    return lax.psum_scatter(partial_value, "st", scatter_dimension=1, tiled=True)


VMEM_LIMIT = 24 * 1024 * 1024


def params():
    return pltpu.CompilerParams(vmem_limit_bytes=VMEM_LIMIT)


def in_vmem():
    return pl.BlockSpec(memory_space=pltpu.VMEM)


def in_smem():
    return pl.BlockSpec(memory_space=pltpu.SMEM)


def stay(x):
    return pltpu.with_memory_space_constraint(x, pltpu.HBM)


def in_hbm():
    return pl.BlockSpec(memory_space=pltpu.HBM)


def green_moves(green_ref, buf, sent_ref, sems, out_sems, first, lane):
    rows, size = sent_ref.shape[:2]
    takes, gives = [], []
    for i in range(rows):
        takes.append(
            pltpu.make_async_copy(
                green_ref.at[i, pl.ds(first, size), :, pl.ds(lane, LANES)], buf.at[i], sems.at[i]
            )
        )
        gives.append(pltpu.make_async_copy(buf.at[i], sent_ref.at[i], out_sems.at[i]))
    return takes, gives


def first_kernel(
    st_count, side_ref, green_ref, weights_ref, mask_ref, strain_ref,
    sent_ref, masked_ref, pieces_ref,
    buf, weights_buf, mask_buf, pieces_buf, sems, out_sems, strain_sems, pieces_sems, small_sems,
):
    lane = pl.multiple_of((1 - side_ref[0]) * LANES, LANES)
    small = [
        pltpu.make_async_copy(weights_ref, weights_buf, small_sems.at[0]),
        pltpu.make_async_copy(mask_ref, mask_buf, small_sems.at[1]),
    ]
    takes, gives = green_moves(green_ref, buf, sent_ref, sems, out_sems, 0, lane)
    for i in range(pieces_ref.shape[0]):
        lane = pl.multiple_of((i * st_count + side_ref[0]) * LANES, LANES)
        takes.append(
            pltpu.make_async_copy(
                strain_ref.at[:, :, pl.ds(lane, LANES)], pieces_buf.at[i], strain_sems.at[i]
            )
        )
        gives.append(pltpu.make_async_copy(pieces_buf.at[i], pieces_ref.at[i], pieces_sems.at[i]))
    for copy in small + takes:
        copy.start()
    for copy in small:
        copy.wait()
    keep = mask_buf[...].astype(jnp.bfloat16)
    for r in range(2):
        for f in range(3):
            masked_ref[r, f] = weights_buf[r, f] * keep
    for take, give in zip(takes, gives):
        take.wait()
        give.start()
    for copy in gives:
        copy.wait()


def first_pieces(side, green, weights, mask, strain, ev_count, st_count):
    rows, _, stations, _ = green.shape
    parts, events, _ = strain.shape
    sent = (rows, COMPONENTS // 2, stations, LANES)
    pieces = (ev_count, parts, events, LANES)
    return pl.pallas_call(
        functools.partial(first_kernel, st_count),
        out_shape=(
            jax.ShapeDtypeStruct(sent, green.dtype),
            jax.ShapeDtypeStruct(weights.shape, weights.dtype),
            jax.ShapeDtypeStruct(pieces, strain.dtype),
        ),
        in_specs=[in_smem(), in_hbm(), in_hbm(), in_hbm(), in_hbm()],
        out_specs=(in_hbm(), in_vmem(), in_hbm()),
        scratch_shapes=[
            pltpu.VMEM(sent, green.dtype),
            pltpu.VMEM(weights.shape, weights.dtype),
            pltpu.VMEM(mask.shape, mask.dtype),
            pltpu.VMEM(pieces, strain.dtype),
            pltpu.SemaphoreType.DMA((rows,)),
            pltpu.SemaphoreType.DMA((rows,)),
            pltpu.SemaphoreType.DMA((ev_count,)),
            pltpu.SemaphoreType.DMA((ev_count,)),
            pltpu.SemaphoreType.DMA((2,)),
        ],
        compiler_params=params(),
        name="first_pieces",
    )(side, stay(green), stay(weights), stay(mask), stay(strain))


def green_kernel(side_ref, green_ref, sent_ref, buf, sems, out_sems):
    lane = pl.multiple_of((1 - side_ref[0]) * LANES, LANES)
    takes, gives = green_moves(green_ref, buf, sent_ref, sems, out_sems, COMPONENTS // 2, lane)
    for take in takes:
        take.start()
    for take, give in zip(takes, gives):
        take.wait()
        give.start()
    for give in gives:
        give.wait()


def green_pieces(side, green):
    rows, _, stations, _ = green.shape
    shape = (rows, COMPONENTS // 2, stations, LANES)
    return pl.pallas_call(
        green_kernel,
        out_shape=jax.ShapeDtypeStruct(shape, green.dtype),
        in_specs=[in_smem(), in_hbm()],
        out_specs=in_hbm(),
        scratch_shapes=[
            pltpu.VMEM(shape, green.dtype),
            pltpu.SemaphoreType.DMA((rows,)),
            pltpu.SemaphoreType.DMA((rows,)),
        ],
        compiler_params=params(),
        name="green_pieces",
    )(side, stay(green))


def own_kernel(side_ref, green_ref, own_ref, sems):
    lane = pl.multiple_of(side_ref[0] * LANES, LANES)
    copies = [
        pltpu.make_async_copy(green_ref.at[i, :, :, pl.ds(lane, LANES)], own_ref.at[i], sems.at[i])
        for i in range(own_ref.shape[0])
    ]
    for copy in copies:
        copy.start()
    for copy in copies:
        copy.wait()


def own_green(side, green):
    rows, parts, stations, _ = green.shape
    return pl.pallas_call(
        own_kernel,
        out_shape=jax.ShapeDtypeStruct((rows, parts, stations, LANES), green.dtype),
        in_specs=[in_smem(), in_hbm()],
        out_specs=in_vmem(),
        scratch_shapes=[pltpu.SemaphoreType.DMA((rows,))],
        compiler_params=params(),
        name="own_green",
    )(side, stay(green))


def stacked(block_ref, components):
    columns = [
        jnp.concatenate([block_ref[i, c] for i in range(block_ref.shape[0])], axis=0)
        for c in components
    ]
    return columns[0] if len(columns) == 1 else jnp.concatenate(columns, axis=1)


def turned(block_ref, c):
    kinds = block_ref.shape[0] // 2
    real = jnp.concatenate([block_ref[i, c] for i in range(kinds)], axis=0)
    imag = jnp.concatenate([block_ref[kinds + i, c] for i in range(kinds)], axis=0)
    upper = jnp.concatenate([real, imag], axis=1)
    lower = jnp.concatenate([-imag, real], axis=1)
    return jnp.concatenate([upper, lower], axis=0)


def product(left, right):
    return jnp.dot(left, right, preferred_element_type=jnp.float32)


def held_half(w_refs, own_ref, other_ref, held_ref, before_ref, rows_ref, lhs):
    _, far, _, _, events, stations = w_refs[0].shape
    half = 2 * far * events
    for k, w_ref in enumerate(w_refs):
        for z in range(far):
            start = (k * far + z) * events
            rows = slice(start, start + events)
            low = slice(half + start, half + start + events)
            for f in range(3):
                first = slice(f * stations, (f + 1) * stations)
                second = slice((3 + f) * stations, (4 + f) * stations)
                for h in range(2):
                    real = w_ref[h, z, 0, f]
                    imag = w_ref[h, z, 1, f]
                    lhs[h, rows, first] = real
                    lhs[h, low, first] = imag
                    lhs[h, rows, second] = -imag
                    lhs[h, low, second] = real
                rows_ref[rows, first] = real
                rows_ref[rows, second] = imag
    wide = 2 * LANES
    held_ref[:, :wide] = product(lhs[0], stacked(own_ref, (0, 1))) + product(
        lhs[1], stacked(other_ref, (0, 1))
    )
    middle = product(lhs[0], stacked(own_ref, (2, 3)))
    held_ref[:, wide:] = middle[:, :LANES] + product(lhs[1], stacked(other_ref, (2,)))
    before_ref[:, :LANES] = middle[:, LANES:]
    before_ref[:, LANES:] = product(lhs[0], stacked(own_ref, (4, 5)))


def held_kernel(near_ref, core_ref, own_ref, other_ref, held_ref, before_ref, rows_ref, lhs):
    held_half((near_ref, core_ref), own_ref, other_ref, held_ref, before_ref, rows_ref, lhs)


def held(near, core, own, other):
    _, far, _, _, events, stations = near.shape
    rows = 4 * far * events
    part = jax.ShapeDtypeStruct((rows, 3 * LANES), jnp.float32)
    return pl.pallas_call(
        held_kernel,
        out_shape=(part, part, jax.ShapeDtypeStruct((rows // 2, 6 * stations), jnp.bfloat16)),
        in_specs=[in_vmem()] * 4,
        out_specs=(in_vmem(),) * 3,
        scratch_shapes=[pltpu.VMEM((2, rows, 6 * stations), jnp.bfloat16)],
        compiler_params=params(),
    )(near, core, own, other)


def rest_kernel(
    rows_a_ref, rows_b_ref, held_a_ref, held_b_ref, before_a_ref, before_b_ref, other_ref,
    full_ref, left,
):
    half = rows_a_ref.shape[0]
    base = held_a_ref.shape[1]
    full_ref[0, :, :base] = held_a_ref[...]
    full_ref[1, :, :base] = held_b_ref[...]
    left[:half] = rows_a_ref[...]
    left[half:] = rows_b_ref[...]
    for c in range(COMPONENTS // 2):
        lanes = slice(c * LANES, (c + 1) * LANES)
        fresh = product(left[...], turned(other_ref, c))
        for y, before_ref in enumerate((before_a_ref, before_b_ref)):
            mine = slice(y * half, (y + 1) * half)
            out = slice(base + c * LANES, base + (c + 1) * LANES)
            full_ref[y, :half, out] = before_ref[:half, lanes] + fresh[mine, :LANES]
            full_ref[y, half:, out] = before_ref[half:, lanes] + fresh[mine, LANES:]


def held_rest(rows_a, rows_b, held_a, held_b, before_a, before_b, other):
    half, depth = rows_a.shape
    return pl.pallas_call(
        rest_kernel,
        out_shape=jax.ShapeDtypeStruct((2, 2 * half, COMPONENTS * LANES), jnp.float32),
        in_specs=[in_vmem()] * 7,
        out_specs=in_vmem(),
        scratch_shapes=[pltpu.VMEM((2 * half, depth), rows_a.dtype)],
        compiler_params=params(),
        name="held_rest",
    )(rows_a, rows_b, held_a, held_b, before_a, before_b, other)


def combine_kernel(bits, me_ref, strain_ref, full_ref, o_ref):
    count, _, events, _ = strain_ref.shape
    far = count // 4
    half = count // 2 * events
    trace = jnp.zeros((events, LANES), jnp.float32)
    normal = jnp.zeros((events, LANES), jnp.float32)
    cross = jnp.zeros((events, LANES), jnp.float32)
    for y in range(2):
        for k in range(2):
            for z in range(far):
                offset = y * 2 + k + sum(bit for place, bit in enumerate(bits) if z >> place & 1)
                block = me_ref[0] ^ offset
                start = (k * far + z) * events
                rows = slice(start, start + events)
                low = slice(half + start, half + start + events)
                sums = None
                for c in range(COMPONENTS):
                    real = strain_ref[block, c].astype(jnp.float32)
                    imag = strain_ref[block, COMPONENTS + c].astype(jnp.float32)
                    lanes = slice(c * LANES, (c + 1) * LANES)
                    held_real = full_ref[y, rows, lanes]
                    held_imag = full_ref[y, low, lanes]
                    term = real * held_real - imag * held_imag
                    if c < 3:
                        normal = normal + term
                        four = (real, imag, held_real, held_imag)
                        sums = four if sums is None else tuple(u + v for u, v in zip(sums, four))
                    else:
                        cross = cross + term
                trace = trace + (sums[0] * sums[2] - sums[1] * sums[3])
    o_ref[0:1, :] = jnp.sum(trace, axis=0, keepdims=True)
    o_ref[1:2, :] = jnp.sum(normal + 2.0 * cross, axis=0, keepdims=True)


def combine(bits, me, strain, full):
    return pl.pallas_call(
        functools.partial(combine_kernel, bits),
        out_shape=jax.ShapeDtypeStruct((2, LANES), jnp.float32),
        in_specs=[in_smem()] + [in_vmem()] * 2,
        out_specs=in_vmem(),
        compiler_params=params(),
        name="combine",
    )(me, strain, full)


def paired(strain, green, weights, mask):
    return paired_steps(strain, green, weights, mask)


def paired_steps(strain, green, weights, mask):
    ev_count = lax.axis_size("ev")
    st_count = lax.axis_size("st")
    event_rows = strain.shape[2]
    station_count = green.shape[2]
    me = lax.axis_index("ev").astype(jnp.int32)[None]
    side = lax.axis_index("st").astype(jnp.int32)[None]

    def hop(x, bit):
        return lax.ppermute(x, "ev", [(i, i ^ bit) for i in range(ev_count)])

    def swap(x):
        return lax.ppermute(x, "st", [(0, 1), (1, 0)])

    green = jnp.transpose(green, (0, 1, 3, 2, 4)).reshape(6, COMPONENTS, station_count, 2 * LANES)
    sent_first, masked, pieces = first_pieces(
        side, green, weights, mask, strain.reshape(12, event_rows, -1), ev_count, st_count
    )
    other_first = swap(sent_first)
    gathered, bits = masked[None], []
    bit = ev_count // 2
    while bit > 2:
        gathered = jnp.concatenate([gathered, hop(gathered, bit)])
        bits.append(bit)
        bit //= 2
    moved = lax.all_to_all(pieces, "ev", 0, 0, tiled=True)

    near = jnp.stack([gathered, swap(gathered)])
    sent_rest = green_pieces(side, green)
    other_rest = swap(sent_rest)
    y = hop(near, 2)
    core = hop(near, 1)
    both = hop(y, 1)

    own = own_green(side, green)
    held_a, before_a, rows_a = held(near, core, own, other_first)
    held_b, before_b, rows_b = held(y, both, own, other_first)
    full = held_rest(rows_a, rows_b, held_a, held_b, before_a, before_b, other_rest)
    return combine(bits, me, moved, full)


def local(strain, green, weights, mask):
    ev_count = lax.axis_size("ev")
    st_count = lax.axis_size("st")
    fits = (
        st_count == 2
        and ev_count >= 8
        and ev_count & (ev_count - 1) == 0
        and green.shape[4] == st_count * LANES
        and green.shape[2] % LANES == 0
        and strain.shape[2] % 16 == 0
    )
    return (paired if fits else general)(strain, green, weights, mask)


def solution(mesh):
    placed = (
        P(None, None, "ev", None),
        P(None, None, "st", None, "ev"),
        P(None, None, "ev", "st"),
        P("ev", "st"),
    )
    return jax.shard_map(
        local, mesh=mesh, in_specs=placed, out_specs=P(None, ("ev", "st")), check_vma=False
    )
```

```python
import functools

import jax
import jax.numpy as jnp
from jax import lax
from jax.experimental import pallas as pl
from jax.experimental.pallas import tpu as pltpu
from jax.sharding import PartitionSpec as P

LANES = 128
COMPONENTS = 6


def general(strain, green, weights, mask):
    masked = weights * mask.astype(jnp.bfloat16)[None, None]
    cells_dev = green.shape[4]
    station_count = green.shape[2]
    event_rows = strain.shape[2]
    ev_count = lax.axis_size("ev")
    st_count = lax.axis_size("st")
    sub_cells = cells_dev // st_count
    shaped = strain.reshape(2, 6, event_rows, ev_count, st_count, sub_cells)
    selected = lax.dynamic_index_in_dim(shaped, lax.axis_index("st"), 4, keepdims=False)
    selected = selected.reshape(2, 6, event_rows, ev_count * sub_cells)
    narrow = lax.all_to_all(selected, "ev", split_axis=3, concat_axis=2, tiled=True)
    strain_all = lax.all_gather(narrow, "st", axis=3, tiled=True)
    green_flat = green.reshape(2, 3, station_count, 6 * cells_dev)
    voigt = jnp.array([1.0, 1.0, 1.0, 2.0, 2.0, 2.0], jnp.float32)
    weight_rows = lax.all_gather(masked, "ev", axis=2, tiled=True)
    row_count = weight_rows.shape[2]
    products = jnp.einsum(
        "rfps,qfsn->rqpn", weight_rows, green_flat, preferred_element_type=jnp.float32
    )
    held_real = (products[0, 0] - products[1, 1]).reshape(row_count, 6, cells_dev)
    held_imag = (products[0, 1] + products[1, 0]).reshape(row_count, 6, cells_dev)
    strain_rows = strain_all.astype(jnp.float32)
    strain_real = jnp.swapaxes(strain_rows[0], 0, 1)
    strain_imag = jnp.swapaxes(strain_rows[1], 0, 1)
    trace_term = jnp.sum(
        strain_real[:, :3].sum(1) * held_real[:, :3].sum(1)
        - strain_imag[:, :3].sum(1) * held_imag[:, :3].sum(1),
        axis=0,
    )
    shear_term = jnp.sum(
        (strain_real * held_real - strain_imag * held_imag) * voigt[None, :, None], axis=(0, 1)
    )
    partial_value = jnp.stack([trace_term, shear_term])
    return lax.psum_scatter(partial_value, "st", scatter_dimension=1, tiled=True)


VMEM_LIMIT = 24 * 1024 * 1024


def params():
    return pltpu.CompilerParams(vmem_limit_bytes=VMEM_LIMIT)


def in_vmem():
    return pl.BlockSpec(memory_space=pltpu.VMEM)


def in_smem():
    return pl.BlockSpec(memory_space=pltpu.SMEM)


def stay(x):
    return pltpu.with_memory_space_constraint(x, pltpu.HBM)


def in_hbm():
    return pl.BlockSpec(memory_space=pltpu.HBM)


def green_moves(green_ref, buf, sent_ref, sems, out_sems, first, lane):
    rows, size = sent_ref.shape[:2]
    takes, gives = [], []
    for i in range(rows):
        takes.append(
            pltpu.make_async_copy(
                green_ref.at[i, pl.ds(first, size), :, pl.ds(lane, LANES)], buf.at[i], sems.at[i]
            )
        )
        gives.append(pltpu.make_async_copy(buf.at[i], sent_ref.at[i], out_sems.at[i]))
    return takes, gives


def first_kernel(
    st_count, side_ref, green_ref, weights_ref, mask_ref, strain_ref,
    sent_ref, masked_ref, pieces_ref,
    buf, weights_buf, mask_buf, pieces_buf, sems, out_sems, strain_sems, pieces_sems, small_sems,
):
    lane = pl.multiple_of((1 - side_ref[0]) * LANES, LANES)
    small = [
        pltpu.make_async_copy(weights_ref, weights_buf, small_sems.at[0]),
        pltpu.make_async_copy(mask_ref, mask_buf, small_sems.at[1]),
    ]
    takes, gives = green_moves(green_ref, buf, sent_ref, sems, out_sems, 0, lane)
    for i in range(pieces_ref.shape[0]):
        lane = pl.multiple_of((i * st_count + side_ref[0]) * LANES, LANES)
        takes.append(
            pltpu.make_async_copy(
                strain_ref.at[:, :, pl.ds(lane, LANES)], pieces_buf.at[i], strain_sems.at[i]
            )
        )
        gives.append(pltpu.make_async_copy(pieces_buf.at[i], pieces_ref.at[i], pieces_sems.at[i]))
    for copy in small + takes:
        copy.start()
    for copy in small:
        copy.wait()
    keep = mask_buf[...].astype(jnp.bfloat16)
    for r in range(2):
        for f in range(3):
            masked_ref[r, f] = weights_buf[r, f] * keep
    for take, give in zip(takes, gives):
        take.wait()
        give.start()
    for copy in gives:
        copy.wait()


def first_pieces(side, green, weights, mask, strain, ev_count, st_count):
    rows, _, stations, _ = green.shape
    parts, events, _ = strain.shape
    sent = (rows, COMPONENTS // 2, stations, LANES)
    pieces = (ev_count, parts, events, LANES)
    return pl.pallas_call(
        functools.partial(first_kernel, st_count),
        out_shape=(
            jax.ShapeDtypeStruct(sent, green.dtype),
            jax.ShapeDtypeStruct(weights.shape, weights.dtype),
            jax.ShapeDtypeStruct(pieces, strain.dtype),
        ),
        in_specs=[in_smem(), in_hbm(), in_hbm(), in_hbm(), in_hbm()],
        out_specs=(in_hbm(), in_vmem(), in_hbm()),
        scratch_shapes=[
            pltpu.VMEM(sent, green.dtype),
            pltpu.VMEM(weights.shape, weights.dtype),
            pltpu.VMEM(mask.shape, mask.dtype),
            pltpu.VMEM(pieces, strain.dtype),
            pltpu.SemaphoreType.DMA((rows,)),
            pltpu.SemaphoreType.DMA((rows,)),
            pltpu.SemaphoreType.DMA((ev_count,)),
            pltpu.SemaphoreType.DMA((ev_count,)),
            pltpu.SemaphoreType.DMA((2,)),
        ],
        compiler_params=params(),
        name="first_pieces",
    )(side, stay(green), stay(weights), stay(mask), stay(strain))


def green_kernel(side_ref, green_ref, sent_ref, buf, sems, out_sems):
    lane = pl.multiple_of((1 - side_ref[0]) * LANES, LANES)
    takes, gives = green_moves(green_ref, buf, sent_ref, sems, out_sems, COMPONENTS // 2, lane)
    for take in takes:
        take.start()
    for take, give in zip(takes, gives):
        take.wait()
        give.start()
    for give in gives:
        give.wait()


def green_pieces(side, green):
    rows, _, stations, _ = green.shape
    shape = (rows, COMPONENTS // 2, stations, LANES)
    return pl.pallas_call(
        green_kernel,
        out_shape=jax.ShapeDtypeStruct(shape, green.dtype),
        in_specs=[in_smem(), in_hbm()],
        out_specs=in_hbm(),
        scratch_shapes=[
            pltpu.VMEM(shape, green.dtype),
            pltpu.SemaphoreType.DMA((rows,)),
            pltpu.SemaphoreType.DMA((rows,)),
        ],
        compiler_params=params(),
        name="green_pieces",
    )(side, stay(green))


def own_kernel(side_ref, green_ref, own_ref, sems):
    lane = pl.multiple_of(side_ref[0] * LANES, LANES)
    copies = [
        pltpu.make_async_copy(green_ref.at[i, :, :, pl.ds(lane, LANES)], own_ref.at[i], sems.at[i])
        for i in range(own_ref.shape[0])
    ]
    for copy in copies:
        copy.start()
    for copy in copies:
        copy.wait()


def own_green(side, green):
    rows, parts, stations, _ = green.shape
    return pl.pallas_call(
        own_kernel,
        out_shape=jax.ShapeDtypeStruct((rows, parts, stations, LANES), green.dtype),
        in_specs=[in_smem(), in_hbm()],
        out_specs=in_vmem(),
        scratch_shapes=[pltpu.SemaphoreType.DMA((rows,))],
        compiler_params=params(),
        name="own_green",
    )(side, stay(green))


def stacked(block_ref, components):
    columns = [
        jnp.concatenate([block_ref[i, c] for i in range(block_ref.shape[0])], axis=0)
        for c in components
    ]
    return columns[0] if len(columns) == 1 else jnp.concatenate(columns, axis=1)


def turned(block_ref, c):
    kinds = block_ref.shape[0] // 2
    real = jnp.concatenate([block_ref[i, c] for i in range(kinds)], axis=0)
    imag = jnp.concatenate([block_ref[kinds + i, c] for i in range(kinds)], axis=0)
    upper = jnp.concatenate([real, imag], axis=1)
    lower = jnp.concatenate([-imag, real], axis=1)
    return jnp.concatenate([upper, lower], axis=0)


def product(left, right):
    return jnp.dot(left, right, preferred_element_type=jnp.float32)


def held_half(w_refs, own_ref, other_ref, held_ref, before_ref, rows_ref, lhs):
    _, far, _, _, events, stations = w_refs[0].shape
    half = 2 * far * events
    for k, w_ref in enumerate(w_refs):
        for z in range(far):
            start = (k * far + z) * events
            rows = slice(start, start + events)
            low = slice(half + start, half + start + events)
            for f in range(3):
                first = slice(f * stations, (f + 1) * stations)
                second = slice((3 + f) * stations, (4 + f) * stations)
                for h in range(2):
                    real = w_ref[h, z, 0, f]
                    imag = w_ref[h, z, 1, f]
                    lhs[h, rows, first] = real
                    lhs[h, low, first] = imag
                    lhs[h, rows, second] = -imag
                    lhs[h, low, second] = real
                rows_ref[rows, first] = real
                rows_ref[rows, second] = imag
    wide = 2 * LANES
    held_ref[:, :wide] = product(lhs[0], stacked(own_ref, (0, 1))) + product(
        lhs[1], stacked(other_ref, (0, 1))
    )
    middle = product(lhs[0], stacked(own_ref, (2, 3)))
    held_ref[:, wide:] = middle[:, :LANES] + product(lhs[1], stacked(other_ref, (2,)))
    before_ref[:, :LANES] = middle[:, LANES:]
    before_ref[:, LANES:] = product(lhs[0], stacked(own_ref, (4, 5)))


def held_kernel(near_ref, core_ref, own_ref, other_ref, held_ref, before_ref, rows_ref, lhs):
    held_half((near_ref, core_ref), own_ref, other_ref, held_ref, before_ref, rows_ref, lhs)


def held(near, core, own, other):
    _, far, _, _, events, stations = near.shape
    rows = 4 * far * events
    part = jax.ShapeDtypeStruct((rows, 3 * LANES), jnp.float32)
    return pl.pallas_call(
        held_kernel,
        out_shape=(part, part, jax.ShapeDtypeStruct((rows // 2, 6 * stations), jnp.bfloat16)),
        in_specs=[in_vmem()] * 4,
        out_specs=(in_vmem(),) * 3,
        scratch_shapes=[pltpu.VMEM((2, rows, 6 * stations), jnp.bfloat16)],
        compiler_params=params(),
    )(near, core, own, other)


def rest_kernel(
    rows_a_ref, rows_b_ref, held_a_ref, held_b_ref, before_a_ref, before_b_ref, other_ref,
    full_ref, left,
):
    half = rows_a_ref.shape[0]
    base = held_a_ref.shape[1]
    full_ref[0, :, :base] = held_a_ref[...]
    full_ref[1, :, :base] = held_b_ref[...]
    left[:half] = rows_a_ref[...]
    left[half:] = rows_b_ref[...]
    for c in range(COMPONENTS // 2):
        lanes = slice(c * LANES, (c + 1) * LANES)
        fresh = product(left[...], turned(other_ref, c))
        for y, before_ref in enumerate((before_a_ref, before_b_ref)):
            mine = slice(y * half, (y + 1) * half)
            out = slice(base + c * LANES, base + (c + 1) * LANES)
            full_ref[y, :half, out] = before_ref[:half, lanes] + fresh[mine, :LANES]
            full_ref[y, half:, out] = before_ref[half:, lanes] + fresh[mine, LANES:]


def held_rest(rows_a, rows_b, held_a, held_b, before_a, before_b, other):
    half, depth = rows_a.shape
    return pl.pallas_call(
        rest_kernel,
        out_shape=jax.ShapeDtypeStruct((2, 2 * half, COMPONENTS * LANES), jnp.float32),
        in_specs=[in_vmem()] * 7,
        out_specs=in_vmem(),
        scratch_shapes=[pltpu.VMEM((2 * half, depth), rows_a.dtype)],
        compiler_params=params(),
        name="held_rest",
    )(rows_a, rows_b, held_a, held_b, before_a, before_b, other)


def combine_kernel(me_ref, strain_ref, full_ref, o_ref):
    count, _, events, _ = strain_ref.shape
    far = count // 4
    half = count // 2 * events
    trace = jnp.zeros((events, LANES), jnp.float32)
    normal = jnp.zeros((events, LANES), jnp.float32)
    cross = jnp.zeros((events, LANES), jnp.float32)
    for y in range(2):
        for k in range(2):
            for z in range(far):
                offset = 4 * z + 2 * y + k
                block = me_ref[0] ^ offset
                start = (k * far + z) * events
                rows = slice(start, start + events)
                low = slice(half + start, half + start + events)
                sums = None
                for c in range(COMPONENTS):
                    real = strain_ref[block, c].astype(jnp.float32)
                    imag = strain_ref[block, COMPONENTS + c].astype(jnp.float32)
                    lanes = slice(c * LANES, (c + 1) * LANES)
                    held_real = full_ref[y, rows, lanes]
                    held_imag = full_ref[y, low, lanes]
                    term = real * held_real - imag * held_imag
                    if c < 3:
                        normal = normal + term
                        four = (real, imag, held_real, held_imag)
                        sums = four if sums is None else tuple(u + v for u, v in zip(sums, four))
                    else:
                        cross = cross + term
                trace = trace + (sums[0] * sums[2] - sums[1] * sums[3])
    o_ref[0:1, :] = jnp.sum(trace, axis=0, keepdims=True)
    o_ref[1:2, :] = jnp.sum(normal + 2.0 * cross, axis=0, keepdims=True)


def combine(me, strain, full):
    return pl.pallas_call(
        combine_kernel,
        out_shape=jax.ShapeDtypeStruct((2, LANES), jnp.float32),
        in_specs=[in_smem()] + [in_vmem()] * 2,
        out_specs=in_vmem(),
        compiler_params=params(),
        name="combine",
    )(me, strain, full)


def paired(strain, green, weights, mask):
    return paired_steps(strain, green, weights, mask)


def paired_steps(strain, green, weights, mask):
    ev_count = lax.axis_size("ev")
    st_count = lax.axis_size("st")
    event_rows = strain.shape[2]
    station_count = green.shape[2]
    me = lax.axis_index("ev").astype(jnp.int32)[None]
    side = lax.axis_index("st").astype(jnp.int32)[None]

    def hop(x, bit):
        return lax.ppermute(x, "ev", [(i, i ^ bit) for i in range(ev_count)])

    def swap(x):
        return lax.ppermute(x, "st", [(0, 1), (1, 0)])

    green = jnp.transpose(green, (0, 1, 3, 2, 4)).reshape(6, COMPONENTS, station_count, 2 * LANES)
    sent_first, masked, pieces = first_pieces(
        side, green, weights, mask, strain.reshape(12, event_rows, -1), ev_count, st_count
    )
    other_first = swap(sent_first)
    gathered = jnp.stack([masked] + [hop(masked, bit) for bit in range(4, ev_count, 4)])
    moved = lax.all_to_all(pieces, "ev", 0, 0, tiled=True)

    near = jnp.stack([gathered, swap(gathered)])
    sent_rest = green_pieces(side, green)
    other_rest = swap(sent_rest)
    y = hop(near, 2)
    core = hop(near, 1)
    both = hop(y, 1)

    own = own_green(side, green)
    held_a, before_a, rows_a = held(near, core, own, other_first)
    held_b, before_b, rows_b = held(y, both, own, other_first)
    full = held_rest(rows_a, rows_b, held_a, held_b, before_a, before_b, other_rest)
    return combine(me, moved, full)


def local(strain, green, weights, mask):
    ev_count = lax.axis_size("ev")
    st_count = lax.axis_size("st")
    fits = (
        st_count == 2
        and ev_count >= 8
        and ev_count & (ev_count - 1) == 0
        and green.shape[4] == st_count * LANES
        and green.shape[2] % LANES == 0
        and strain.shape[2] % 16 == 0
    )
    return (paired if fits else general)(strain, green, weights, mask)


def solution(mesh):
    placed = (
        P(None, None, "ev", None),
        P(None, None, "st", None, "ev"),
        P(None, None, "ev", "st"),
        P("ev", "st"),
    )
    return jax.shard_map(
        local, mesh=mesh, in_specs=placed, out_specs=P(None, ("ev", "st")), check_vma=False
    )
```

```python
import functools

import jax
import jax.numpy as jnp
from jax import lax
from jax.experimental import pallas as pl
from jax.experimental.pallas import tpu as pltpu
from jax.sharding import PartitionSpec as P

LANES = 128
COMPONENTS = 6


def general(strain, green, weights, mask):
    masked = weights * mask.astype(jnp.bfloat16)[None, None]
    cells_dev = green.shape[4]
    station_count = green.shape[2]
    event_rows = strain.shape[2]
    ev_count = lax.axis_size("ev")
    st_count = lax.axis_size("st")
    sub_cells = cells_dev // st_count
    shaped = strain.reshape(2, 6, event_rows, ev_count, st_count, sub_cells)
    selected = lax.dynamic_index_in_dim(shaped, lax.axis_index("st"), 4, keepdims=False)
    selected = selected.reshape(2, 6, event_rows, ev_count * sub_cells)
    narrow = lax.all_to_all(selected, "ev", split_axis=3, concat_axis=2, tiled=True)
    strain_all = lax.all_gather(narrow, "st", axis=3, tiled=True)
    green_flat = green.reshape(2, 3, station_count, 6 * cells_dev)
    voigt = jnp.array([1.0, 1.0, 1.0, 2.0, 2.0, 2.0], jnp.float32)
    weight_rows = lax.all_gather(masked, "ev", axis=2, tiled=True)
    row_count = weight_rows.shape[2]
    products = jnp.einsum(
        "rfps,qfsn->rqpn", weight_rows, green_flat, preferred_element_type=jnp.float32
    )
    held_real = (products[0, 0] - products[1, 1]).reshape(row_count, 6, cells_dev)
    held_imag = (products[0, 1] + products[1, 0]).reshape(row_count, 6, cells_dev)
    strain_rows = strain_all.astype(jnp.float32)
    strain_real = jnp.swapaxes(strain_rows[0], 0, 1)
    strain_imag = jnp.swapaxes(strain_rows[1], 0, 1)
    trace_term = jnp.sum(
        strain_real[:, :3].sum(1) * held_real[:, :3].sum(1)
        - strain_imag[:, :3].sum(1) * held_imag[:, :3].sum(1),
        axis=0,
    )
    shear_term = jnp.sum(
        (strain_real * held_real - strain_imag * held_imag) * voigt[None, :, None], axis=(0, 1)
    )
    partial_value = jnp.stack([trace_term, shear_term])
    return lax.psum_scatter(partial_value, "st", scatter_dimension=1, tiled=True)


VMEM_LIMIT = 24 * 1024 * 1024


def params():
    return pltpu.CompilerParams(vmem_limit_bytes=VMEM_LIMIT)


def in_vmem():
    return pl.BlockSpec(memory_space=pltpu.VMEM)


def in_smem():
    return pl.BlockSpec(memory_space=pltpu.SMEM)


def stay(x):
    return pltpu.with_memory_space_constraint(x, pltpu.HBM)


def in_hbm():
    return pl.BlockSpec(memory_space=pltpu.HBM)


def green_moves(green_ref, buf, sent_ref, sems, out_sems, first, lane):
    rows, size = sent_ref.shape[:2]
    takes, gives = [], []
    for i in range(rows):
        takes.append(
            pltpu.make_async_copy(
                green_ref.at[i, pl.ds(first, size), :, pl.ds(lane, LANES)], buf.at[i], sems.at[i]
            )
        )
        gives.append(pltpu.make_async_copy(buf.at[i], sent_ref.at[i], out_sems.at[i]))
    return takes, gives


def first_kernel(
    st_count, side_ref, green_ref, weights_ref, mask_ref, strain_ref,
    sent_ref, masked_ref, pieces_ref,
    buf, weights_buf, mask_buf, pieces_buf, sems, out_sems, strain_sems, pieces_sems, small_sems,
):
    lane = pl.multiple_of((1 - side_ref[0]) * LANES, LANES)
    small = [
        pltpu.make_async_copy(weights_ref, weights_buf, small_sems.at[0]),
        pltpu.make_async_copy(mask_ref, mask_buf, small_sems.at[1]),
    ]
    takes, gives = green_moves(green_ref, buf, sent_ref, sems, out_sems, 0, lane)
    for i in range(pieces_ref.shape[0]):
        lane = pl.multiple_of((i * st_count + side_ref[0]) * LANES, LANES)
        takes.append(
            pltpu.make_async_copy(
                strain_ref.at[:, :, pl.ds(lane, LANES)], pieces_buf.at[i], strain_sems.at[i]
            )
        )
        gives.append(pltpu.make_async_copy(pieces_buf.at[i], pieces_ref.at[i], pieces_sems.at[i]))
    count = sems.shape[0]
    priorities = [0] * count + [1] * (len(takes) - count)
    for copy in small:
        copy.start()
    for copy, priority in zip(takes, priorities):
        copy.start(priority=priority)
    for copy in small:
        copy.wait()
    keep = mask_buf[...].astype(jnp.bfloat16)
    for r in range(2):
        for f in range(3):
            masked_ref[r, f] = weights_buf[r, f] * keep
    for take, give, priority in zip(takes, gives, priorities):
        take.wait()
        give.start(priority=priority)
    for copy in gives:
        copy.wait()


def first_pieces(side, green, weights, mask, strain, ev_count, st_count):
    rows, _, stations, _ = green.shape
    parts, events, _ = strain.shape
    sent = (rows, COMPONENTS // 2, stations, LANES)
    pieces = (ev_count, parts, events, LANES)
    return pl.pallas_call(
        functools.partial(first_kernel, st_count),
        out_shape=(
            jax.ShapeDtypeStruct(sent, green.dtype),
            jax.ShapeDtypeStruct(weights.shape, weights.dtype),
            jax.ShapeDtypeStruct(pieces, strain.dtype),
        ),
        in_specs=[in_smem(), in_hbm(), in_hbm(), in_hbm(), in_hbm()],
        out_specs=(in_hbm(), in_vmem(), in_hbm()),
        scratch_shapes=[
            pltpu.VMEM(sent, green.dtype),
            pltpu.VMEM(weights.shape, weights.dtype),
            pltpu.VMEM(mask.shape, mask.dtype),
            pltpu.VMEM(pieces, strain.dtype),
            pltpu.SemaphoreType.DMA((rows,)),
            pltpu.SemaphoreType.DMA((rows,)),
            pltpu.SemaphoreType.DMA((ev_count,)),
            pltpu.SemaphoreType.DMA((ev_count,)),
            pltpu.SemaphoreType.DMA((2,)),
        ],
        compiler_params=params(),
        name="first_pieces",
    )(side, stay(green), stay(weights), stay(mask), stay(strain))


def green_kernel(side_ref, green_ref, sent_ref, buf, sems, out_sems):
    lane = pl.multiple_of((1 - side_ref[0]) * LANES, LANES)
    takes, gives = green_moves(green_ref, buf, sent_ref, sems, out_sems, COMPONENTS // 2, lane)
    for take in takes:
        take.start()
    for take, give in zip(takes, gives):
        take.wait()
        give.start()
    for give in gives:
        give.wait()


def green_pieces(side, green):
    rows, _, stations, _ = green.shape
    shape = (rows, COMPONENTS // 2, stations, LANES)
    return pl.pallas_call(
        green_kernel,
        out_shape=jax.ShapeDtypeStruct(shape, green.dtype),
        in_specs=[in_smem(), in_hbm()],
        out_specs=in_hbm(),
        scratch_shapes=[
            pltpu.VMEM(shape, green.dtype),
            pltpu.SemaphoreType.DMA((rows,)),
            pltpu.SemaphoreType.DMA((rows,)),
        ],
        compiler_params=params(),
        name="green_pieces",
    )(side, stay(green))


def own_kernel(side_ref, green_ref, own_ref, sems):
    lane = pl.multiple_of(side_ref[0] * LANES, LANES)
    copies = [
        pltpu.make_async_copy(green_ref.at[i, :, :, pl.ds(lane, LANES)], own_ref.at[i], sems.at[i])
        for i in range(own_ref.shape[0])
    ]
    for copy in copies:
        copy.start()
    for copy in copies:
        copy.wait()


def own_green(side, green):
    rows, parts, stations, _ = green.shape
    return pl.pallas_call(
        own_kernel,
        out_shape=jax.ShapeDtypeStruct((rows, parts, stations, LANES), green.dtype),
        in_specs=[in_smem(), in_hbm()],
        out_specs=in_vmem(),
        scratch_shapes=[pltpu.SemaphoreType.DMA((rows,))],
        compiler_params=params(),
        name="own_green",
    )(side, stay(green))


def stacked(block_ref, components):
    columns = [
        jnp.concatenate([block_ref[i, c] for i in range(block_ref.shape[0])], axis=0)
        for c in components
    ]
    return columns[0] if len(columns) == 1 else jnp.concatenate(columns, axis=1)


def turned(block_ref, c):
    kinds = block_ref.shape[0] // 2
    real = jnp.concatenate([block_ref[i, c] for i in range(kinds)], axis=0)
    imag = jnp.concatenate([block_ref[kinds + i, c] for i in range(kinds)], axis=0)
    upper = jnp.concatenate([real, imag], axis=1)
    lower = jnp.concatenate([-imag, real], axis=1)
    return jnp.concatenate([upper, lower], axis=0)


def product(left, right):
    return jnp.dot(left, right, preferred_element_type=jnp.float32)


def held_half(w_refs, own_ref, other_ref, held_ref, before_ref, rows_ref, lhs):
    _, far, _, _, events, stations = w_refs[0].shape
    half = 2 * far * events
    for k, w_ref in enumerate(w_refs):
        for z in range(far):
            start = (k * far + z) * events
            rows = slice(start, start + events)
            low = slice(half + start, half + start + events)
            for f in range(3):
                first = slice(f * stations, (f + 1) * stations)
                second = slice((3 + f) * stations, (4 + f) * stations)
                for h in range(2):
                    real = w_ref[h, z, 0, f]
                    imag = w_ref[h, z, 1, f]
                    lhs[h, rows, first] = real
                    lhs[h, low, first] = imag
                    lhs[h, rows, second] = -imag
                    lhs[h, low, second] = real
                rows_ref[rows, first] = real
                rows_ref[rows, second] = imag
    wide = 2 * LANES
    held_ref[:, :wide] = product(lhs[0], stacked(own_ref, (0, 1))) + product(
        lhs[1], stacked(other_ref, (0, 1))
    )
    middle = product(lhs[0], stacked(own_ref, (2, 3)))
    held_ref[:, wide:] = middle[:, :LANES] + product(lhs[1], stacked(other_ref, (2,)))
    before_ref[:, :LANES] = middle[:, LANES:]
    before_ref[:, LANES:] = product(lhs[0], stacked(own_ref, (4, 5)))


def held_kernel(near_ref, core_ref, own_ref, other_ref, held_ref, before_ref, rows_ref, lhs):
    held_half((near_ref, core_ref), own_ref, other_ref, held_ref, before_ref, rows_ref, lhs)


def held(near, core, own, other):
    _, far, _, _, events, stations = near.shape
    rows = 4 * far * events
    part = jax.ShapeDtypeStruct((rows, 3 * LANES), jnp.float32)
    return pl.pallas_call(
        held_kernel,
        out_shape=(part, part, jax.ShapeDtypeStruct((rows // 2, 6 * stations), jnp.bfloat16)),
        in_specs=[in_vmem()] * 4,
        out_specs=(in_vmem(),) * 3,
        scratch_shapes=[pltpu.VMEM((2, rows, 6 * stations), jnp.bfloat16)],
        compiler_params=params(),
    )(near, core, own, other)


def rest_kernel(
    rows_a_ref, rows_b_ref, held_a_ref, held_b_ref, before_a_ref, before_b_ref, other_ref,
    full_ref, left,
):
    half = rows_a_ref.shape[0]
    base = held_a_ref.shape[1]
    full_ref[0, :, :base] = held_a_ref[...]
    full_ref[1, :, :base] = held_b_ref[...]
    left[:half] = rows_a_ref[...]
    left[half:] = rows_b_ref[...]
    for c in range(COMPONENTS // 2):
        lanes = slice(c * LANES, (c + 1) * LANES)
        fresh = product(left[...], turned(other_ref, c))
        for y, before_ref in enumerate((before_a_ref, before_b_ref)):
            mine = slice(y * half, (y + 1) * half)
            out = slice(base + c * LANES, base + (c + 1) * LANES)
            full_ref[y, :half, out] = before_ref[:half, lanes] + fresh[mine, :LANES]
            full_ref[y, half:, out] = before_ref[half:, lanes] + fresh[mine, LANES:]


def held_rest(rows_a, rows_b, held_a, held_b, before_a, before_b, other):
    half, depth = rows_a.shape
    return pl.pallas_call(
        rest_kernel,
        out_shape=jax.ShapeDtypeStruct((2, 2 * half, COMPONENTS * LANES), jnp.float32),
        in_specs=[in_vmem()] * 7,
        out_specs=in_vmem(),
        scratch_shapes=[pltpu.VMEM((2 * half, depth), rows_a.dtype)],
        compiler_params=params(),
        name="held_rest",
    )(rows_a, rows_b, held_a, held_b, before_a, before_b, other)


def combine_kernel(me_ref, strain_ref, full_ref, o_ref):
    count, _, events, _ = strain_ref.shape
    far = count // 4
    half = count // 2 * events
    trace = jnp.zeros((events, LANES), jnp.float32)
    normal = jnp.zeros((events, LANES), jnp.float32)
    cross = jnp.zeros((events, LANES), jnp.float32)
    for y in range(2):
        for k in range(2):
            for z in range(far):
                offset = 4 * z + 2 * y + k
                block = me_ref[0] ^ offset
                start = (k * far + z) * events
                rows = slice(start, start + events)
                low = slice(half + start, half + start + events)
                sums = None
                for c in range(COMPONENTS):
                    real = strain_ref[block, c].astype(jnp.float32)
                    imag = strain_ref[block, COMPONENTS + c].astype(jnp.float32)
                    lanes = slice(c * LANES, (c + 1) * LANES)
                    held_real = full_ref[y, rows, lanes]
                    held_imag = full_ref[y, low, lanes]
                    term = real * held_real - imag * held_imag
                    if c < 3:
                        normal = normal + term
                        four = (real, imag, held_real, held_imag)
                        sums = four if sums is None else tuple(u + v for u, v in zip(sums, four))
                    else:
                        cross = cross + term
                trace = trace + (sums[0] * sums[2] - sums[1] * sums[3])
    o_ref[0:1, :] = jnp.sum(trace, axis=0, keepdims=True)
    o_ref[1:2, :] = jnp.sum(normal + 2.0 * cross, axis=0, keepdims=True)


def combine(me, strain, full):
    return pl.pallas_call(
        combine_kernel,
        out_shape=jax.ShapeDtypeStruct((2, LANES), jnp.float32),
        in_specs=[in_smem()] + [in_vmem()] * 2,
        out_specs=in_vmem(),
        compiler_params=params(),
        name="combine",
    )(me, strain, full)


def paired(strain, green, weights, mask):
    return paired_steps(strain, green, weights, mask)


def paired_steps(strain, green, weights, mask):
    ev_count = lax.axis_size("ev")
    st_count = lax.axis_size("st")
    event_rows = strain.shape[2]
    station_count = green.shape[2]
    me = lax.axis_index("ev").astype(jnp.int32)[None]
    side = lax.axis_index("st").astype(jnp.int32)[None]

    def hop(x, bit):
        return lax.ppermute(x, "ev", [(i, i ^ bit) for i in range(ev_count)])

    def swap(x):
        return lax.ppermute(x, "st", [(0, 1), (1, 0)])

    green = jnp.transpose(green, (0, 1, 3, 2, 4)).reshape(6, COMPONENTS, station_count, 2 * LANES)
    sent_first, masked, pieces = first_pieces(
        side, green, weights, mask, strain.reshape(12, event_rows, -1), ev_count, st_count
    )
    other_first = swap(sent_first)
    gathered = jnp.stack([masked] + [hop(masked, bit) for bit in range(4, ev_count, 4)])
    moved = lax.all_to_all(pieces, "ev", 0, 0, tiled=True)

    partner = swap(gathered)
    near = jnp.stack([gathered, partner])
    sent_rest = green_pieces(side, green)
    other_rest = swap(sent_rest)
    y = jnp.stack([hop(gathered, 2), hop(partner, 2)])
    core = hop(near, 1)
    both = hop(y, 1)

    own = own_green(side, green)
    held_a, before_a, rows_a = held(near, core, own, other_first)
    held_b, before_b, rows_b = held(y, both, own, other_first)
    full = held_rest(rows_a, rows_b, held_a, held_b, before_a, before_b, other_rest)
    return combine(me, moved, full)


def local(strain, green, weights, mask):
    ev_count = lax.axis_size("ev")
    st_count = lax.axis_size("st")
    fits = (
        st_count == 2
        and ev_count >= 8
        and ev_count & (ev_count - 1) == 0
        and green.shape[4] == st_count * LANES
        and green.shape[2] % LANES == 0
        and strain.shape[2] % 16 == 0
    )
    return (paired if fits else general)(strain, green, weights, mask)


def solution(mesh):
    placed = (
        P(None, None, "ev", None),
        P(None, None, "st", None, "ev"),
        P(None, None, "ev", "st"),
        P("ev", "st"),
    )
    return jax.shard_map(
        local, mesh=mesh, in_specs=placed, out_specs=P(None, ("ev", "st")), check_vma=False
    )
```

```python
import functools

import jax
import jax.numpy as jnp
from jax import lax
from jax.experimental import pallas as pl
from jax.experimental.pallas import tpu as pltpu
from jax.sharding import PartitionSpec as P

LANES = 128
COMPONENTS = 6


def general(strain, green, weights, mask):
    masked = weights * mask.astype(jnp.bfloat16)[None, None]
    cells_dev = green.shape[4]
    station_count = green.shape[2]
    event_rows = strain.shape[2]
    ev_count = lax.axis_size("ev")
    st_count = lax.axis_size("st")
    sub_cells = cells_dev // st_count
    shaped = strain.reshape(2, 6, event_rows, ev_count, st_count, sub_cells)
    selected = lax.dynamic_index_in_dim(shaped, lax.axis_index("st"), 4, keepdims=False)
    selected = selected.reshape(2, 6, event_rows, ev_count * sub_cells)
    narrow = lax.all_to_all(selected, "ev", split_axis=3, concat_axis=2, tiled=True)
    strain_all = lax.all_gather(narrow, "st", axis=3, tiled=True)
    green_flat = green.reshape(2, 3, station_count, 6 * cells_dev)
    voigt = jnp.array([1.0, 1.0, 1.0, 2.0, 2.0, 2.0], jnp.float32)
    weight_rows = lax.all_gather(masked, "ev", axis=2, tiled=True)
    row_count = weight_rows.shape[2]
    products = jnp.einsum(
        "rfps,qfsn->rqpn", weight_rows, green_flat, preferred_element_type=jnp.float32
    )
    held_real = (products[0, 0] - products[1, 1]).reshape(row_count, 6, cells_dev)
    held_imag = (products[0, 1] + products[1, 0]).reshape(row_count, 6, cells_dev)
    strain_rows = strain_all.astype(jnp.float32)
    strain_real = jnp.swapaxes(strain_rows[0], 0, 1)
    strain_imag = jnp.swapaxes(strain_rows[1], 0, 1)
    trace_term = jnp.sum(
        strain_real[:, :3].sum(1) * held_real[:, :3].sum(1)
        - strain_imag[:, :3].sum(1) * held_imag[:, :3].sum(1),
        axis=0,
    )
    shear_term = jnp.sum(
        (strain_real * held_real - strain_imag * held_imag) * voigt[None, :, None], axis=(0, 1)
    )
    partial_value = jnp.stack([trace_term, shear_term])
    return lax.psum_scatter(partial_value, "st", scatter_dimension=1, tiled=True)


VMEM_LIMIT = 24 * 1024 * 1024


def params():
    return pltpu.CompilerParams(vmem_limit_bytes=VMEM_LIMIT)


def in_vmem():
    return pl.BlockSpec(memory_space=pltpu.VMEM)


def in_smem():
    return pl.BlockSpec(memory_space=pltpu.SMEM)


def stay(x):
    return pltpu.with_memory_space_constraint(x, pltpu.HBM)


def in_hbm():
    return pl.BlockSpec(memory_space=pltpu.HBM)


def green_moves(green_ref, buf, sent_ref, sems, out_sems, first, lane):
    rows, size = sent_ref.shape[:2]
    takes, gives = [], []
    for i in range(rows):
        takes.append(
            pltpu.make_async_copy(
                green_ref.at[i, pl.ds(first, size), :, pl.ds(lane, LANES)], buf.at[i], sems.at[i]
            )
        )
        gives.append(pltpu.make_async_copy(buf.at[i], sent_ref.at[i], out_sems.at[i]))
    return takes, gives


def first_kernel(
    st_count, side_ref, green_ref, weights_ref, mask_ref, strain_ref,
    sent_ref, masked_ref, pieces_ref,
    buf, weights_buf, mask_buf, pieces_buf, sems, out_sems, strain_sems, pieces_sems, small_sems,
):
    lane = pl.multiple_of((1 - side_ref[0]) * LANES, LANES)
    small = [
        pltpu.make_async_copy(weights_ref, weights_buf, small_sems.at[0]),
        pltpu.make_async_copy(mask_ref, mask_buf, small_sems.at[1]),
    ]
    takes, gives = green_moves(green_ref, buf, sent_ref, sems, out_sems, 0, lane)
    for i in range(pieces_ref.shape[0]):
        lane = pl.multiple_of((i * st_count + side_ref[0]) * LANES, LANES)
        takes.append(
            pltpu.make_async_copy(
                strain_ref.at[:, :, pl.ds(lane, LANES)], pieces_buf.at[i], strain_sems.at[i]
            )
        )
        gives.append(pltpu.make_async_copy(pieces_buf.at[i], pieces_ref.at[i], pieces_sems.at[i]))
    count = sems.shape[0]
    priorities = [0] * count + [1] * (len(takes) - count)
    for copy in small:
        copy.start()
    for copy, priority in zip(takes, priorities):
        copy.start(priority=priority)
    for copy in small:
        copy.wait()
    keep = mask_buf[...].astype(jnp.bfloat16)
    for r in range(2):
        for f in range(3):
            masked_ref[r, f] = weights_buf[r, f] * keep
    for take, give, priority in zip(takes, gives, priorities):
        take.wait()
        give.start(priority=priority)
    for copy in gives:
        copy.wait()


def first_pieces(side, green, weights, mask, strain, ev_count, st_count):
    rows, _, stations, _ = green.shape
    parts, events, _ = strain.shape
    sent = (rows, COMPONENTS // 2, stations, LANES)
    pieces = (ev_count, parts, events, LANES)
    return pl.pallas_call(
        functools.partial(first_kernel, st_count),
        out_shape=(
            jax.ShapeDtypeStruct(sent, green.dtype),
            jax.ShapeDtypeStruct(weights.shape, weights.dtype),
            jax.ShapeDtypeStruct(pieces, strain.dtype),
        ),
        in_specs=[in_smem(), in_hbm(), in_hbm(), in_hbm(), in_hbm()],
        out_specs=(in_hbm(), in_vmem(), in_hbm()),
        scratch_shapes=[
            pltpu.VMEM(sent, green.dtype),
            pltpu.VMEM(weights.shape, weights.dtype),
            pltpu.VMEM(mask.shape, mask.dtype),
            pltpu.VMEM(pieces, strain.dtype),
            pltpu.SemaphoreType.DMA((rows,)),
            pltpu.SemaphoreType.DMA((rows,)),
            pltpu.SemaphoreType.DMA((ev_count,)),
            pltpu.SemaphoreType.DMA((ev_count,)),
            pltpu.SemaphoreType.DMA((2,)),
        ],
        compiler_params=params(),
        name="first_pieces",
    )(side, stay(green), stay(weights), stay(mask), stay(strain))


def green_kernel(side_ref, green_ref, sent_ref, buf, sems, out_sems):
    lane = pl.multiple_of((1 - side_ref[0]) * LANES, LANES)
    takes, gives = green_moves(green_ref, buf, sent_ref, sems, out_sems, COMPONENTS // 2, lane)
    for take in takes:
        take.start()
    for take, give in zip(takes, gives):
        take.wait()
        give.start()
    for give in gives:
        give.wait()


def green_pieces(side, green):
    rows, _, stations, _ = green.shape
    shape = (rows, COMPONENTS // 2, stations, LANES)
    return pl.pallas_call(
        green_kernel,
        out_shape=jax.ShapeDtypeStruct(shape, green.dtype),
        in_specs=[in_smem(), in_hbm()],
        out_specs=in_hbm(),
        scratch_shapes=[
            pltpu.VMEM(shape, green.dtype),
            pltpu.SemaphoreType.DMA((rows,)),
            pltpu.SemaphoreType.DMA((rows,)),
        ],
        compiler_params=params(),
        name="green_pieces",
    )(side, stay(green))


def own_kernel(side_ref, green_ref, own_ref, sems):
    lane = pl.multiple_of(side_ref[0] * LANES, LANES)
    copies = [
        pltpu.make_async_copy(green_ref.at[i, :, :, pl.ds(lane, LANES)], own_ref.at[i], sems.at[i])
        for i in range(own_ref.shape[0])
    ]
    for copy in copies:
        copy.start()
    for copy in copies:
        copy.wait()


def own_green(side, green):
    rows, parts, stations, _ = green.shape
    return pl.pallas_call(
        own_kernel,
        out_shape=jax.ShapeDtypeStruct((rows, parts, stations, LANES), green.dtype),
        in_specs=[in_smem(), in_hbm()],
        out_specs=in_vmem(),
        scratch_shapes=[pltpu.SemaphoreType.DMA((rows,))],
        compiler_params=params(),
        name="own_green",
    )(side, stay(green))


def stacked(block_ref, components):
    columns = [
        jnp.concatenate([block_ref[i, c] for i in range(block_ref.shape[0])], axis=0)
        for c in components
    ]
    return columns[0] if len(columns) == 1 else jnp.concatenate(columns, axis=1)


def turned(block_ref, c):
    kinds = block_ref.shape[0] // 2
    real = jnp.concatenate([block_ref[i, c] for i in range(kinds)], axis=0)
    imag = jnp.concatenate([block_ref[kinds + i, c] for i in range(kinds)], axis=0)
    upper = jnp.concatenate([real, imag], axis=1)
    lower = jnp.concatenate([-imag, real], axis=1)
    return jnp.concatenate([upper, lower], axis=0)


def product(left, right):
    return jnp.dot(left, right, preferred_element_type=jnp.float32)


def held_half(w_refs, own_ref, other_ref, held_ref, before_ref, rows_ref, lhs):
    _, far, _, _, events, stations = w_refs[0].shape
    half = 2 * far * events
    for k, w_ref in enumerate(w_refs):
        for z in range(far):
            start = (k * far + z) * events
            rows = slice(start, start + events)
            low = slice(half + start, half + start + events)
            for f in range(3):
                first = slice(f * stations, (f + 1) * stations)
                second = slice((3 + f) * stations, (4 + f) * stations)
                for h in range(2):
                    real = w_ref[h, z, 0, f]
                    imag = w_ref[h, z, 1, f]
                    lhs[h, rows, first] = real
                    lhs[h, low, first] = imag
                    lhs[h, rows, second] = -imag
                    lhs[h, low, second] = real
                rows_ref[rows, first] = real
                rows_ref[rows, second] = imag
    wide = 2 * LANES
    held_ref[:, :wide] = product(lhs[0], stacked(own_ref, (0, 1))) + product(
        lhs[1], stacked(other_ref, (0, 1))
    )
    middle = product(lhs[0], stacked(own_ref, (2, 3)))
    held_ref[:, wide:] = middle[:, :LANES] + product(lhs[1], stacked(other_ref, (2,)))
    before_ref[:, :LANES] = middle[:, LANES:]
    before_ref[:, LANES:] = product(lhs[0], stacked(own_ref, (4, 5)))


def held_kernel(near_ref, core_ref, own_ref, other_ref, held_ref, before_ref, rows_ref, lhs):
    held_half((near_ref, core_ref), own_ref, other_ref, held_ref, before_ref, rows_ref, lhs)


def held(near, core, own, other):
    _, far, _, _, events, stations = near.shape
    rows = 4 * far * events
    part = jax.ShapeDtypeStruct((rows, 3 * LANES), jnp.float32)
    return pl.pallas_call(
        held_kernel,
        out_shape=(part, part, jax.ShapeDtypeStruct((rows // 2, 6 * stations), jnp.bfloat16)),
        in_specs=[in_vmem()] * 4,
        out_specs=(in_vmem(),) * 3,
        scratch_shapes=[pltpu.VMEM((2, rows, 6 * stations), jnp.bfloat16)],
        compiler_params=params(),
    )(near, core, own, other)


def rest_kernel(
    rows_a_ref, rows_b_ref, held_a_ref, held_b_ref, before_a_ref, before_b_ref, other_ref,
    full_ref,
):
    half = rows_a_ref.shape[0]
    base = held_a_ref.shape[1]
    left = jnp.concatenate([rows_a_ref[...], rows_b_ref[...]], axis=0)
    full_ref[0, :, :base] = held_a_ref[...]
    full_ref[1, :, :base] = held_b_ref[...]
    for c in range(COMPONENTS // 2):
        lanes = slice(c * LANES, (c + 1) * LANES)
        fresh = product(left, turned(other_ref, c))
        for y, before_ref in enumerate((before_a_ref, before_b_ref)):
            mine = slice(y * half, (y + 1) * half)
            out = slice(base + c * LANES, base + (c + 1) * LANES)
            full_ref[y, :half, out] = before_ref[:half, lanes] + fresh[mine, :LANES]
            full_ref[y, half:, out] = before_ref[half:, lanes] + fresh[mine, LANES:]


def held_rest(rows_a, rows_b, held_a, held_b, before_a, before_b, other):
    half = rows_a.shape[0]
    return pl.pallas_call(
        rest_kernel,
        out_shape=jax.ShapeDtypeStruct((2, 2 * half, COMPONENTS * LANES), jnp.float32),
        in_specs=[in_vmem()] * 7,
        out_specs=in_vmem(),
        compiler_params=params(),
        name="held_rest",
    )(rows_a, rows_b, held_a, held_b, before_a, before_b, other)


def combine_kernel(me_ref, strain_ref, full_ref, o_ref):
    count, _, events, _ = strain_ref.shape
    far = count // 4
    half = count // 2 * events
    trace = jnp.zeros((events, LANES), jnp.float32)
    normal = jnp.zeros((events, LANES), jnp.float32)
    cross = jnp.zeros((events, LANES), jnp.float32)
    for y in range(2):
        for k in range(2):
            for z in range(far):
                offset = 4 * z + 2 * y + k
                block = me_ref[0] ^ offset
                start = (k * far + z) * events
                rows = slice(start, start + events)
                low = slice(half + start, half + start + events)
                sums = None
                for c in range(COMPONENTS):
                    real = strain_ref[block, c].astype(jnp.float32)
                    imag = strain_ref[block, COMPONENTS + c].astype(jnp.float32)
                    lanes = slice(c * LANES, (c + 1) * LANES)
                    held_real = full_ref[y, rows, lanes]
                    held_imag = full_ref[y, low, lanes]
                    term = real * held_real - imag * held_imag
                    if c < 3:
                        normal = normal + term
                        four = (real, imag, held_real, held_imag)
                        sums = four if sums is None else tuple(u + v for u, v in zip(sums, four))
                    else:
                        cross = cross + term
                trace = trace + (sums[0] * sums[2] - sums[1] * sums[3])
    o_ref[0:1, :] = jnp.sum(trace, axis=0, keepdims=True)
    o_ref[1:2, :] = jnp.sum(normal + 2.0 * cross, axis=0, keepdims=True)


def combine(me, strain, full):
    return pl.pallas_call(
        combine_kernel,
        out_shape=jax.ShapeDtypeStruct((2, LANES), jnp.float32),
        in_specs=[in_smem()] + [in_vmem()] * 2,
        out_specs=in_vmem(),
        compiler_params=params(),
        name="combine",
    )(me, strain, full)


def paired(strain, green, weights, mask):
    return paired_steps(strain, green, weights, mask)


def paired_steps(strain, green, weights, mask):
    ev_count = lax.axis_size("ev")
    st_count = lax.axis_size("st")
    event_rows = strain.shape[2]
    station_count = green.shape[2]
    me = lax.axis_index("ev").astype(jnp.int32)[None]
    side = lax.axis_index("st").astype(jnp.int32)[None]

    def hop(x, bit):
        return lax.ppermute(x, "ev", [(i, i ^ bit) for i in range(ev_count)])

    def swap(x):
        return lax.ppermute(x, "st", [(0, 1), (1, 0)])

    green = jnp.transpose(green, (0, 1, 3, 2, 4)).reshape(6, COMPONENTS, station_count, 2 * LANES)
    sent_first, masked, pieces = first_pieces(
        side, green, weights, mask, strain.reshape(12, event_rows, -1), ev_count, st_count
    )
    other_first = swap(sent_first)
    gathered = jnp.stack([masked] + [hop(masked, bit) for bit in range(4, ev_count, 4)])
    moved = lax.all_to_all(pieces, "ev", 0, 0, tiled=True)

    partner = swap(gathered)
    near = jnp.stack([gathered, partner])
    sent_rest = green_pieces(side, green)
    other_rest = swap(sent_rest)
    y = jnp.stack([hop(gathered, 2), hop(partner, 2)])
    core = hop(near, 1)
    both = hop(y, 1)

    own = own_green(side, green)
    held_a, before_a, rows_a = held(near, core, own, other_first)
    held_b, before_b, rows_b = held(y, both, own, other_first)
    full = held_rest(rows_a, rows_b, held_a, held_b, before_a, before_b, other_rest)
    return combine(me, moved, full)


def local(strain, green, weights, mask):
    ev_count = lax.axis_size("ev")
    st_count = lax.axis_size("st")
    fits = (
        st_count == 2
        and ev_count >= 8
        and ev_count & (ev_count - 1) == 0
        and green.shape[4] == st_count * LANES
        and green.shape[2] % LANES == 0
        and strain.shape[2] % 16 == 0
    )
    return (paired if fits else general)(strain, green, weights, mask)


def solution(mesh):
    placed = (
        P(None, None, "ev", None),
        P(None, None, "st", None, "ev"),
        P(None, None, "ev", "st"),
        P("ev", "st"),
    )
    return jax.shard_map(
        local, mesh=mesh, in_specs=placed, out_specs=P(None, ("ev", "st")), check_vma=False
    )
```

```python
import functools

import jax
import jax.numpy as jnp
from jax import lax
from jax.experimental import pallas as pl
from jax.experimental.pallas import tpu as pltpu
from jax.sharding import PartitionSpec as P

LANES = 128
COMPONENTS = 6


def general(strain, green, weights, mask):
    masked = weights * mask.astype(jnp.bfloat16)[None, None]
    cells_dev = green.shape[4]
    station_count = green.shape[2]
    event_rows = strain.shape[2]
    ev_count = lax.axis_size("ev")
    st_count = lax.axis_size("st")
    sub_cells = cells_dev // st_count
    shaped = strain.reshape(2, 6, event_rows, ev_count, st_count, sub_cells)
    selected = lax.dynamic_index_in_dim(shaped, lax.axis_index("st"), 4, keepdims=False)
    selected = selected.reshape(2, 6, event_rows, ev_count * sub_cells)
    narrow = lax.all_to_all(selected, "ev", split_axis=3, concat_axis=2, tiled=True)
    strain_all = lax.all_gather(narrow, "st", axis=3, tiled=True)
    green_flat = green.reshape(2, 3, station_count, 6 * cells_dev)
    voigt = jnp.array([1.0, 1.0, 1.0, 2.0, 2.0, 2.0], jnp.float32)
    weight_rows = lax.all_gather(masked, "ev", axis=2, tiled=True)
    row_count = weight_rows.shape[2]
    products = jnp.einsum(
        "rfps,qfsn->rqpn", weight_rows, green_flat, preferred_element_type=jnp.float32
    )
    held_real = (products[0, 0] - products[1, 1]).reshape(row_count, 6, cells_dev)
    held_imag = (products[0, 1] + products[1, 0]).reshape(row_count, 6, cells_dev)
    strain_rows = strain_all.astype(jnp.float32)
    strain_real = jnp.swapaxes(strain_rows[0], 0, 1)
    strain_imag = jnp.swapaxes(strain_rows[1], 0, 1)
    trace_term = jnp.sum(
        strain_real[:, :3].sum(1) * held_real[:, :3].sum(1)
        - strain_imag[:, :3].sum(1) * held_imag[:, :3].sum(1),
        axis=0,
    )
    shear_term = jnp.sum(
        (strain_real * held_real - strain_imag * held_imag) * voigt[None, :, None], axis=(0, 1)
    )
    partial_value = jnp.stack([trace_term, shear_term])
    return lax.psum_scatter(partial_value, "st", scatter_dimension=1, tiled=True)


VMEM_LIMIT = 24 * 1024 * 1024


def params():
    return pltpu.CompilerParams(vmem_limit_bytes=VMEM_LIMIT)


def in_vmem():
    return pl.BlockSpec(memory_space=pltpu.VMEM)


def in_smem():
    return pl.BlockSpec(memory_space=pltpu.SMEM)


def stay(x):
    return pltpu.with_memory_space_constraint(x, pltpu.HBM)


def in_hbm():
    return pl.BlockSpec(memory_space=pltpu.HBM)


def green_moves(green_ref, buf, sent_ref, sems, out_sems, first, lane):
    rows, size = sent_ref.shape[:2]
    takes, gives = [], []
    for i in range(rows):
        takes.append(
            pltpu.make_async_copy(
                green_ref.at[i, pl.ds(first, size), :, pl.ds(lane, LANES)], buf.at[i], sems.at[i]
            )
        )
        gives.append(pltpu.make_async_copy(buf.at[i], sent_ref.at[i], out_sems.at[i]))
    return takes, gives


def first_kernel(
    st_count, side_ref, green_ref, weights_ref, mask_ref, strain_ref,
    sent_ref, masked_ref, pieces_ref,
    buf, weights_buf, mask_buf, pieces_buf, sems, out_sems, strain_sems, pieces_sems, small_sems,
):
    lane = pl.multiple_of((1 - side_ref[0]) * LANES, LANES)
    small = [
        pltpu.make_async_copy(weights_ref, weights_buf, small_sems.at[0]),
        pltpu.make_async_copy(mask_ref, mask_buf, small_sems.at[1]),
    ]
    takes, gives = green_moves(green_ref, buf, sent_ref, sems, out_sems, 0, lane)
    for i in range(pieces_ref.shape[0]):
        lane = pl.multiple_of((i * st_count + side_ref[0]) * LANES, LANES)
        takes.append(
            pltpu.make_async_copy(
                strain_ref.at[:, :, pl.ds(lane, LANES)], pieces_buf.at[i], strain_sems.at[i]
            )
        )
        gives.append(pltpu.make_async_copy(pieces_buf.at[i], pieces_ref.at[i], pieces_sems.at[i]))
    count = sems.shape[0]
    priorities = [0] * count + [1] * (len(takes) - count)
    for copy in small:
        copy.start()
    for copy, priority in zip(takes, priorities):
        copy.start(priority=priority)
    for copy in small:
        copy.wait()
    keep = mask_buf[...].astype(jnp.bfloat16)
    for r in range(2):
        for f in range(3):
            masked_ref[r, f] = weights_buf[r, f] * keep
    for take, give, priority in zip(takes, gives, priorities):
        take.wait()
        give.start(priority=priority)
    for copy in gives:
        copy.wait()


def first_pieces(side, green, weights, mask, strain, ev_count, st_count):
    rows, _, stations, _ = green.shape
    parts, events, _ = strain.shape
    sent = (rows, COMPONENTS // 2, stations, LANES)
    pieces = (ev_count, parts, events, LANES)
    return pl.pallas_call(
        functools.partial(first_kernel, st_count),
        out_shape=(
            jax.ShapeDtypeStruct(sent, green.dtype),
            jax.ShapeDtypeStruct(weights.shape, weights.dtype),
            jax.ShapeDtypeStruct(pieces, strain.dtype),
        ),
        in_specs=[in_smem(), in_hbm(), in_hbm(), in_hbm(), in_hbm()],
        out_specs=(in_hbm(), in_vmem(), in_hbm()),
        scratch_shapes=[
            pltpu.VMEM(sent, green.dtype),
            pltpu.VMEM(weights.shape, weights.dtype),
            pltpu.VMEM(mask.shape, mask.dtype),
            pltpu.VMEM(pieces, strain.dtype),
            pltpu.SemaphoreType.DMA((rows,)),
            pltpu.SemaphoreType.DMA((rows,)),
            pltpu.SemaphoreType.DMA((ev_count,)),
            pltpu.SemaphoreType.DMA((ev_count,)),
            pltpu.SemaphoreType.DMA((2,)),
        ],
        compiler_params=params(),
        name="first_pieces",
    )(side, stay(green), stay(weights), stay(mask), stay(strain))


def green_kernel(side_ref, green_ref, *refs):
    sent_refs, bufs, sems, out_sems = refs[:2], refs[2:4], refs[4:6], refs[6:8]
    lane = pl.multiple_of((1 - side_ref[0]) * LANES, LANES)
    takes, gives, first = [], [], COMPONENTS // 2
    for k, sent_ref in enumerate(sent_refs):
        more = green_moves(green_ref, bufs[k], sent_ref, sems[k], out_sems[k], first, lane)
        takes += more[0]
        gives += more[1]
        first += sent_ref.shape[1]
    for take in takes:
        take.start()
    for take, give in zip(takes, gives):
        take.wait()
        give.start()
    for give in gives:
        give.wait()


def green_pieces(side, green):
    rows, _, stations, _ = green.shape
    shapes = [(rows, n, stations, LANES) for n in (COMPONENTS // 2 - 1, 1)]
    return pl.pallas_call(
        green_kernel,
        out_shape=tuple(jax.ShapeDtypeStruct(shape, green.dtype) for shape in shapes),
        in_specs=[in_smem(), in_hbm()],
        out_specs=(in_hbm(), in_hbm()),
        scratch_shapes=[pltpu.VMEM(shape, green.dtype) for shape in shapes]
        + [pltpu.SemaphoreType.DMA((rows,))] * 4,
        compiler_params=params(),
        name="green_pieces",
    )(side, stay(green))


def own_kernel(side_ref, green_ref, own_ref, sems):
    lane = pl.multiple_of(side_ref[0] * LANES, LANES)
    copies = [
        pltpu.make_async_copy(green_ref.at[i, :, :, pl.ds(lane, LANES)], own_ref.at[i], sems.at[i])
        for i in range(own_ref.shape[0])
    ]
    for copy in copies:
        copy.start()
    for copy in copies:
        copy.wait()


def own_green(side, green):
    rows, parts, stations, _ = green.shape
    return pl.pallas_call(
        own_kernel,
        out_shape=jax.ShapeDtypeStruct((rows, parts, stations, LANES), green.dtype),
        in_specs=[in_smem(), in_hbm()],
        out_specs=in_vmem(),
        scratch_shapes=[pltpu.SemaphoreType.DMA((rows,))],
        compiler_params=params(),
        name="own_green",
    )(side, stay(green))


def stacked(block_ref, components):
    columns = [
        jnp.concatenate([block_ref[i, c] for i in range(block_ref.shape[0])], axis=0)
        for c in components
    ]
    return columns[0] if len(columns) == 1 else jnp.concatenate(columns, axis=1)


def turned(block_ref, c):
    kinds = block_ref.shape[0] // 2
    real = jnp.concatenate([block_ref[i, c] for i in range(kinds)], axis=0)
    imag = jnp.concatenate([block_ref[kinds + i, c] for i in range(kinds)], axis=0)
    upper = jnp.concatenate([real, imag], axis=1)
    lower = jnp.concatenate([-imag, real], axis=1)
    return jnp.concatenate([upper, lower], axis=0)


def product(left, right):
    return jnp.dot(left, right, preferred_element_type=jnp.float32)


def held_half(w_refs, own_ref, other_ref, held_ref, before_ref, rows_ref, lhs):
    _, far, _, _, events, stations = w_refs[0].shape
    half = 2 * far * events
    for k, w_ref in enumerate(w_refs):
        for z in range(far):
            start = (k * far + z) * events
            rows = slice(start, start + events)
            low = slice(half + start, half + start + events)
            for f in range(3):
                first = slice(f * stations, (f + 1) * stations)
                second = slice((3 + f) * stations, (4 + f) * stations)
                for h in range(2):
                    real = w_ref[h, z, 0, f]
                    imag = w_ref[h, z, 1, f]
                    lhs[h, rows, first] = real
                    lhs[h, low, first] = imag
                    lhs[h, rows, second] = -imag
                    lhs[h, low, second] = real
                rows_ref[rows, first] = real
                rows_ref[rows, second] = imag
    wide = 2 * LANES
    held_ref[:, :wide] = product(lhs[0], stacked(own_ref, (0, 1))) + product(
        lhs[1], stacked(other_ref, (0, 1))
    )
    middle = product(lhs[0], stacked(own_ref, (2, 3)))
    held_ref[:, wide:] = middle[:, :LANES] + product(lhs[1], stacked(other_ref, (2,)))
    before_ref[:, :LANES] = middle[:, LANES:]
    before_ref[:, LANES:] = product(lhs[0], stacked(own_ref, (4, 5)))


def held_kernel(near_ref, core_ref, own_ref, other_ref, held_ref, before_ref, rows_ref, lhs):
    held_half((near_ref, core_ref), own_ref, other_ref, held_ref, before_ref, rows_ref, lhs)


def far_kernel(
    near_ref, core_ref, own_ref, other_ref, mid_ref, near_rows_ref, near_before_ref,
    held_ref, before_ref, rows_ref, more_ref, lhs,
):
    held_half((near_ref, core_ref), own_ref, other_ref, held_ref, before_ref, rows_ref, lhs)
    half = near_rows_ref.shape[0]
    size = mid_ref.shape[1]
    before_ref[:, : size * LANES] += product(lhs[1], stacked(mid_ref, tuple(range(size))))
    for c in range(size):
        lanes = slice(c * LANES, (c + 1) * LANES)
        fresh = product(near_rows_ref[...], turned(mid_ref, c))
        more_ref[:half, lanes] = near_before_ref[:half, lanes] + fresh[:, :LANES]
        more_ref[half:, lanes] = near_before_ref[half:, lanes] + fresh[:, LANES:]


def held(near, core, own, other, *extra):
    _, far, _, _, events, stations = near.shape
    rows = 4 * far * events
    part = jax.ShapeDtypeStruct((rows, 3 * LANES), jnp.float32)
    out = [part, part, jax.ShapeDtypeStruct((rows // 2, 6 * stations), jnp.bfloat16)]
    if extra:
        out.append(jax.ShapeDtypeStruct((rows, 2 * LANES), jnp.float32))
    return pl.pallas_call(
        far_kernel if extra else held_kernel,
        out_shape=tuple(out),
        in_specs=[in_vmem()] * (4 + len(extra)),
        out_specs=(in_vmem(),) * len(out),
        scratch_shapes=[pltpu.VMEM((2, rows, 6 * stations), jnp.bfloat16)],
        compiler_params=params(),
    )(near, core, own, other, *extra)


def rest_kernel(
    rows_a_ref, rows_b_ref, held_a_ref, held_b_ref, before_a_ref, before_b_ref, more_ref, other_ref,
    full_ref,
):
    half = rows_a_ref.shape[0]
    base = held_a_ref.shape[1]
    last = before_a_ref.shape[1] - LANES
    left = jnp.concatenate([rows_a_ref[...], rows_b_ref[...]], axis=0)
    fresh = product(left, turned(other_ref, 0))
    full_ref[0, :, :base] = held_a_ref[...]
    full_ref[0, :, base : base + last] = more_ref[...]
    full_ref[1, :, :base] = held_b_ref[...]
    full_ref[1, :, base : base + last] = before_b_ref[:, :last]
    for y, before_ref in enumerate((before_a_ref, before_b_ref)):
        mine = slice(y * half, (y + 1) * half)
        full_ref[y, :half, base + last :] = before_ref[:half, last:] + fresh[mine, :LANES]
        full_ref[y, half:, base + last :] = before_ref[half:, last:] + fresh[mine, LANES:]


def held_rest(rows_a, rows_b, held_a, held_b, before_a, before_b, more, other):
    half = rows_a.shape[0]
    return pl.pallas_call(
        rest_kernel,
        out_shape=jax.ShapeDtypeStruct((2, 2 * half, COMPONENTS * LANES), jnp.float32),
        in_specs=[in_vmem()] * 8,
        out_specs=in_vmem(),
        compiler_params=params(),
        name="held_rest",
    )(rows_a, rows_b, held_a, held_b, before_a, before_b, more, other)


def combine_kernel(me_ref, strain_ref, full_ref, o_ref):
    count, _, events, _ = strain_ref.shape
    far = count // 4
    half = count // 2 * events
    trace = jnp.zeros((events, LANES), jnp.float32)
    normal = jnp.zeros((events, LANES), jnp.float32)
    cross = jnp.zeros((events, LANES), jnp.float32)
    for y in range(2):
        for k in range(2):
            for z in range(far):
                offset = 4 * z + 2 * y + k
                block = me_ref[0] ^ offset
                start = (k * far + z) * events
                rows = slice(start, start + events)
                low = slice(half + start, half + start + events)
                sums = None
                for c in range(COMPONENTS):
                    real = strain_ref[block, c].astype(jnp.float32)
                    imag = strain_ref[block, COMPONENTS + c].astype(jnp.float32)
                    lanes = slice(c * LANES, (c + 1) * LANES)
                    held_real = full_ref[y, rows, lanes]
                    held_imag = full_ref[y, low, lanes]
                    term = real * held_real - imag * held_imag
                    if c < 3:
                        normal = normal + term
                        four = (real, imag, held_real, held_imag)
                        sums = four if sums is None else tuple(u + v for u, v in zip(sums, four))
                    else:
                        cross = cross + term
                trace = trace + (sums[0] * sums[2] - sums[1] * sums[3])
    o_ref[0:1, :] = jnp.sum(trace, axis=0, keepdims=True)
    o_ref[1:2, :] = jnp.sum(normal + 2.0 * cross, axis=0, keepdims=True)


def combine(me, strain, full):
    return pl.pallas_call(
        combine_kernel,
        out_shape=jax.ShapeDtypeStruct((2, LANES), jnp.float32),
        in_specs=[in_smem()] + [in_vmem()] * 2,
        out_specs=in_vmem(),
        compiler_params=params(),
        name="combine",
    )(me, strain, full)


def paired(strain, green, weights, mask):
    return paired_steps(strain, green, weights, mask)


def paired_steps(strain, green, weights, mask):
    ev_count = lax.axis_size("ev")
    st_count = lax.axis_size("st")
    event_rows = strain.shape[2]
    station_count = green.shape[2]
    me = lax.axis_index("ev").astype(jnp.int32)[None]
    side = lax.axis_index("st").astype(jnp.int32)[None]

    def hop(x, bit):
        return lax.ppermute(x, "ev", [(i, i ^ bit) for i in range(ev_count)])

    def swap(x):
        return lax.ppermute(x, "st", [(0, 1), (1, 0)])

    green = jnp.transpose(green, (0, 1, 3, 2, 4)).reshape(6, COMPONENTS, station_count, 2 * LANES)
    sent_first, masked, pieces = first_pieces(
        side, green, weights, mask, strain.reshape(12, event_rows, -1), ev_count, st_count
    )
    other_first = swap(sent_first)
    gathered = jnp.stack([masked] + [hop(masked, bit) for bit in range(4, ev_count, 4)])
    moved = lax.all_to_all(pieces, "ev", 0, 0, tiled=True)

    partner = swap(gathered)
    near = jnp.stack([gathered, partner])
    sent_mid, sent_last = green_pieces(side, green)
    other_mid = swap(sent_mid)
    other_last = swap(sent_last)
    y = jnp.stack([hop(gathered, 2), hop(partner, 2)])
    core = hop(near, 1)
    both = hop(y, 1)

    own = own_green(side, green)
    held_a, before_a, rows_a = held(near, core, own, other_first)
    held_b, before_b, rows_b, more = held(y, both, own, other_first, other_mid, rows_a, before_a)
    full = held_rest(
        rows_a, rows_b, held_a, held_b, before_a, before_b, more, other_last
    )
    return combine(me, moved, full)


def local(strain, green, weights, mask):
    ev_count = lax.axis_size("ev")
    st_count = lax.axis_size("st")
    fits = (
        st_count == 2
        and ev_count >= 8
        and ev_count & (ev_count - 1) == 0
        and green.shape[4] == st_count * LANES
        and green.shape[2] % LANES == 0
        and strain.shape[2] % 16 == 0
    )
    return (paired if fits else general)(strain, green, weights, mask)


def solution(mesh):
    placed = (
        P(None, None, "ev", None),
        P(None, None, "st", None, "ev"),
        P(None, None, "ev", "st"),
        P("ev", "st"),
    )
    return jax.shard_map(
        local, mesh=mesh, in_specs=placed, out_specs=P(None, ("ev", "st")), check_vma=False
    )
```
